512 devices in a mesh: depth: 4 (over z_hi, core), plane: 128 (over x, z_lo, y).
Axes of the slice: x: 4, y: 4, z: 16 (z_hi: 2, z_lo: 8; z = z_hi * 8 + z_lo), core: 2. Of those that a mesh axis runs over, the one named last changes fastest.
Arguments:
- magnet: float32 [3, 32, 512, 1024], P(None, 'depth', 'plane'), may hold values from -1 to 1, as said below
- mask: int32 [512, 1024], P('plane'), may hold values 0 or 1
- materials: int32 [32], P('depth'), may hold values from 0 to 3
- exchange_strength: float32 [4], replicated, may hold values from 0.5 to 2
- anisotropy: float32 [4], replicated, may hold values from 0.5 to 3
- damping: float32 [4], replicated, may hold values from 0.05 to 0.6
- source_strength: float32 [4], replicated, may hold values from 0.3 to 1.5
- thermal_strength: float32 [4], replicated, may hold values from 0.5 to 2
- pivots: float32 [32, 3, 3], replicated, may hold values from -1 to 1, as said below
- lower: float32 [32, 3, 3], replicated, may hold values from -1 to 1, as said below
- upper: float32 [32, 3, 3], replicated, may hold values from -1 to 1, as said below
- noise_stream: int32 [1], replicated, may hold values from 0 to 999999
- counter: int32 [1], replicated, may hold values from 0 to 99999
Outputs:
- magnet_next: float32 [3, 32, 512, 1024], P(None, 'depth', 'plane')
- accumulation: float32 [3, 32, 512, 1024], P(None, 'depth', 'plane')
The draws below stay inside these ranges and needn't reach their ends.
Inputs may be any that keep to these rules, and one draw needn't show every extreme that they name: `magnet`: unit vectors. `pivots`: each block has spectral norm below 0.98. `lower`: each block has spectral norm below 1. `upper`: each block has spectral norm below 1.
All inputs are finite; a program needn't handle non-finite values. No bound on the sum of `mask` on one device may be relied on, other than what follows from the above.
Results may differ from the reference program's by a relative error of at most 0.000073.
Values sent between devices are 32-bit elements; how exact they have to be, the bound alone decides.
A program may use at most 128 MiB of HBM per device.

```python
import math
import jax
import jax.numpy as jnp
from jax import lax

NY = 1024
NMAT = 4
NX = 512
LZ = 32


def draw_magnet(key, part):
    key_z, key_phi = jax.random.split(key)
    height = jax.random.uniform(key_z, (LZ, NX, NY), jnp.float32, -1.0, 1.0)
    phase = jax.random.uniform(key_phi, (LZ, NX, NY), jnp.float32, -3.14159265, 3.14159265)
    radius = jnp.sqrt(jnp.maximum(1.0 - height * height, 0.0))
    return jnp.stack([radius * jnp.cos(phase), radius * jnp.sin(phase), height]).astype(jnp.float32)


def antisym_blocks(key, diag_lo, diag_hi, sign, spread):
    key_d, key_w = jax.random.split(key)
    diag = sign * jax.random.uniform(key_d, (LZ, 1, 1), jnp.float32, diag_lo, diag_hi)
    twist = jax.random.uniform(key_w, (LZ, 3), jnp.float32, -spread, spread)
    zero = jnp.zeros((LZ,), jnp.float32)
    rows = [jnp.stack([zero, -twist[:, 2], twist[:, 1]], axis=1), jnp.stack([twist[:, 2], zero, -twist[:, 0]], axis=1), jnp.stack([-twist[:, 1], twist[:, 0], zero], axis=1)]
    skew = jnp.stack(rows, axis=1)
    return (diag * jnp.eye(3, dtype=jnp.float32)[None] + skew).astype(jnp.float32)


def draw_pivots(key, part):
    return antisym_blocks(jax.random.fold_in(key, 11), 0.75, 0.95, 1.0, 0.12)


def draw_lower(key, part):
    return antisym_blocks(jax.random.fold_in(key, 23), 0.85, 0.96, -1.0, 0.1)


def draw_upper(key, part):
    return antisym_blocks(jax.random.fold_in(key, 37), 0.75, 0.93, -1.0, 0.12)


def with_ends(values, stream_key, low, largest):
    place = [jax.random.randint(jax.random.fold_in(stream_key, axis), (), 0, length) for axis, length in enumerate(values.shape)]
    longest = values.shape.index(max(values.shape))
    neighbour = place[:longest] + [(place[longest] + 1) % values.shape[longest]] + place[longest + 1:]
    return values.at[tuple(place)].set(low).at[tuple(neighbour)].set(largest)


def setup_inputs(seed: int = 0) -> dict:
    keys = jax.random.split(jax.random.key(seed), 14)
    return {
        "magnet": draw_magnet(jax.random.fold_in(keys[13], 71), 0),
        "mask": with_ends((jax.random.randint(keys[1], (NX, NY), 0, 10) < 9).astype(jnp.int32), jax.random.fold_in(keys[1], 1), 0, 1),
        "materials": with_ends(jax.random.randint(keys[2], (LZ,), 0, NMAT), jax.random.fold_in(keys[2], 1), 0, NMAT - 1).astype(jnp.int32),
        "exchange_strength": jnp.clip(jnp.exp(jax.random.uniform(keys[3], (NMAT,), jnp.float32, math.log(0.5), math.log(2.0))), 0.5, 2.0),
        "anisotropy": jnp.clip(jax.random.uniform(keys[4], (NMAT,), jnp.float32, 0.5, 3.0), 0.5, 3.0),
        "damping": jnp.clip(jax.random.uniform(keys[5], (NMAT,), jnp.float32, 0.05, 0.6), 0.05, 0.6),
        "source_strength": jnp.clip(jax.random.uniform(keys[6], (NMAT,), jnp.float32, 0.3, 1.5), 0.3, 1.5),
        "thermal_strength": jnp.clip(jax.random.uniform(keys[7], (NMAT,), jnp.float32, 0.5, 2.0), 0.5, 2.0),
        "pivots": draw_pivots(jax.random.fold_in(keys[13], 71), 0),
        "lower": draw_lower(jax.random.fold_in(keys[13], 71), 0),
        "upper": draw_upper(jax.random.fold_in(keys[13], 71), 0),
        "noise_stream": jax.random.randint(keys[11], (1,), 0, 1000000).astype(jnp.int32),
        "counter": jax.random.randint(keys[12], (1,), 0, 100000).astype(jnp.int32),
    }


def cross(a, b):
    return jnp.stack([a[1] * b[2] - a[2] * b[1], a[2] * b[0] - a[0] * b[2], a[0] * b[1] - a[1] * b[0]])

def apply_block(block, vec):
    return jnp.stack([block[row, 0] * vec[0] + block[row, 1] * vec[1] + block[row, 2] * vec[2] for row in range(3)])

def solve_columns(source, pivots, lower, upper):
    layer_count = source.shape[1]
    previous = jnp.zeros_like(source[:, 0])
    forward_values = []
    for layer_pos in range(layer_count):
        previous = apply_block(pivots[layer_pos], source[:, layer_pos] - apply_block(lower[layer_pos], previous))
        forward_values.append(previous)
    after = jnp.zeros_like(source[:, 0])
    solved = [None] * layer_count
    for layer_pos in range(layer_count - 1, -1, -1):
        after = forward_values[layer_pos] - apply_block(upper[layer_pos], after)
        solved[layer_pos] = after
    return jnp.stack(solved, axis=1)

def hash_uniform(index, stream, counter):
    mixed = index * 739982445 + stream * 695872825 + counter * 1597334677
    mixed = mixed ^ lax.shift_right_logical(mixed, jnp.int32(16))
    mixed = mixed * 739982445
    mixed = mixed ^ lax.shift_right_logical(mixed, jnp.int32(15))
    mixed = mixed * 695872825
    mixed = mixed ^ lax.shift_right_logical(mixed, jnp.int32(16))
    return (mixed & 65535).astype(jnp.float32) / 32767.5 - 1.0

def layer_values(materials, table):
    onehot = (materials[:, None] == jnp.arange(table.shape[0], dtype=jnp.int32)[None, :]).astype(jnp.float32)
    return lax.optimization_barrier(jnp.sum(onehot * table[None, :], axis=1))[None, :, None, None]

def normalize(vec):
    return vec / jnp.sqrt(lax.optimization_barrier(jnp.sum(vec * vec, axis=0, keepdims=True)))

def reference(magnet, mask, materials, exchange_strength, anisotropy, damping, source_strength, thermal_strength, pivots, lower, upper, noise_stream, counter):
    maskf = mask.astype(jnp.float32)[None, None]
    stiff = layer_values(materials, exchange_strength)
    aniso = layer_values(materials, anisotropy)
    alpha = layer_values(materials, damping)
    beta = layer_values(materials, source_strength)
    theta = layer_values(materials, thermal_strength)
    comp = jnp.arange(3, dtype=jnp.int32)[:, None, None, None]
    layer = jnp.arange(LZ, dtype=jnp.int32)[None, :, None, None]
    xrow = jnp.arange(NX, dtype=jnp.int32)[None, None, :, None]
    ycol = jnp.arange(NY, dtype=jnp.int32)[None, None, None, :]
    index = ((comp * LZ + layer) * NX + xrow) * NY + ycol
    noise = theta * hash_uniform(index, noise_stream[0], counter[0])
    axis_z = jnp.array([0.0, 0.0, 1.0], dtype=jnp.float32)[:, None, None, None]

    def rate(field):
        masked = field * maskf
        near = jnp.roll(masked, 1, 2) + jnp.roll(masked, -1, 2) + jnp.roll(masked, 1, 3) + jnp.roll(masked, -1, 3)
        far = jnp.roll(masked, 2, 2) + jnp.roll(masked, -2, 2) + jnp.roll(masked, 2, 3) + jnp.roll(masked, -2, 3)
        planar = 4.0 / 3.0 * near - 1.0 / 12.0 * far
        padded = jnp.pad(masked, ((0, 0), (1, 1), (0, 0), (0, 0)))
        vertical = padded[:, 2:] + padded[:, :-2]
        accum = solve_columns(beta * field, pivots, lower, upper)
        heff = stiff * (planar + 0.5 * vertical) + aniso * field * axis_z + noise + 0.5 * accum
        torque = cross(field, heff)
        change = -(torque + alpha * cross(field, torque)) / (1.0 + alpha * alpha) * maskf
        return (change, accum)
    first, _ = rate(magnet)
    middle = normalize(magnet + 0.03 * first)
    second, accum = rate(middle)
    magnet_next = normalize(magnet + 0.015 * (first + second))
    return (magnet_next, accum)
```

```python
import functools

import jax
import jax.numpy as jnp
from jax import lax
from jax.experimental import pallas as pl
from jax.experimental.pallas import tpu as pltpu
from jax.sharding import PartitionSpec as P

MESH = pl.DeviceIdType.MESH
LANES = 128
SUB = 8
K1 = 739982445
K2 = 695872825
K3 = 1597334677


def wrap32(value):
    value &= 0xFFFFFFFF
    return value - (1 << 32) if value >= (1 << 31) else value


def cross(a, b):
    return [a[1] * b[2] - a[2] * b[1], a[2] * b[0] - a[0] * b[2], a[0] * b[1] - a[1] * b[0]]


def apply(block, vec):
    return [block[r][0] * vec[0] + block[r][1] * vec[1] + block[r][2] * vec[2] for r in range(3)]


def sub3(a, b):
    return [a[c] - b[c] for c in range(3)]


def add3(a, b):
    return [a[c] + b[c] for c in range(3)]


def shift_right(value, amount):
    return lax.shift_right_logical(value, jnp.full(value.shape, amount, jnp.int32))


def kernel(
    layers,
    rows,
    magnet_ref,
    mask_ref,
    mat_ref,
    stiff_ref,
    aniso_ref,
    damp_ref,
    source_ref,
    theta_ref,
    piv_ref,
    low_ref,
    up_ref,
    stream_ref,
    count_ref,
    next_ref,
    accum_ref,
    base,
    field,
    masked,
    noise,
    rest,
    sweep,
    maskf,
    coef,
    unit_y,
    halo_lo,
    halo_hi,
    edge_lo,
    edge_hi,
    state_out,
    state_in,
    send_sem,
    recv_sem,
):
    depth_id = lax.axis_index("depth")
    plane_id = lax.axis_index("plane")
    depth_count = lax.axis_size("depth")
    plane_count = lax.axis_size("plane")
    total_layers = layers * depth_count
    total_rows = rows * plane_count
    left = lax.rem(plane_id + plane_count - 1, plane_count)
    right = lax.rem(plane_id + 1, plane_count)
    above = depth_id + 1
    below = depth_id - 1
    has_below = depth_id > 0
    has_above = depth_id < depth_count - 1
    first_layer = depth_id * layers

    barrier = pltpu.get_barrier_semaphore()
    pl.semaphore_signal(barrier, inc=1, device_id=(depth_id, left), device_id_type=MESH)
    pl.semaphore_signal(barrier, inc=1, device_id=(depth_id, right), device_id_type=MESH)

    @pl.when(has_below)
    def _():
        pl.semaphore_signal(barrier, inc=1, device_id=(below, plane_id), device_id_type=MESH)

    @pl.when(has_above)
    def _():
        pl.semaphore_signal(barrier, inc=1, device_id=(above, plane_id), device_id_type=MESH)

    lane = lax.broadcasted_iota(jnp.int32, (SUB, LANES), 1)
    sublane = lax.broadcasted_iota(jnp.int32, (SUB, LANES), 0)

    def block_of(ref, layer):
        return [[ref[i, j, layer] for j in range(3)] for i in range(3)]

    for x in range(rows):
        maskf[x] = mask_ref[pl.ds(x, SUB, stride=rows), :].astype(jnp.float32)

    def load_layer(l, carry):
        for c in range(3):
            for x in range(rows):
                value = magnet_ref[c, l, pl.ds(x, SUB, stride=rows), :]
                base[x, l, c] = value
                field[x, l, c] = value
                masked[x, 1 + l, c] = value * maskf[x]
        return carry

    lax.fori_loop(0, layers, load_layer, 0)

    def unit(offset, c):
        return (lane == offset + c).astype(jnp.float32)

    zeros = jnp.zeros((SUB, LANES), jnp.float32)

    def unit_sweep(start, count, inject, finish):
        def down(i, y):
            y = [
                jnp.where(lane // 16 == 1, jnp.where(i == inject, unit(16, c), y[c]), y[c])
                for c in range(3)
            ]
            y = apply(block_of(piv_ref, start + i), apply(block_of(low_ref, start + i), y))
            y = [-y[c] for c in range(3)]
            for c in range(3):
                unit_y[i, c] = y[c]
            return tuple(y)

        last = lax.fori_loop(0, count, down, tuple(unit(0, c) for c in range(3)))

        def up(k, s):
            i = count - 1 - k
            s = apply(block_of(up_ref, start + i), s)
            return tuple(unit_y[i, c] - s[c] for c in range(3))

        mid = lax.fori_loop(0, count - finish, up, tuple(unit(32, c) for c in range(3)))
        first = lax.fori_loop(count - finish, count, up, mid)
        return last, mid, first

    def splat(slot, vec, offset):
        for r in range(3):
            for j in range(3):
                coef[slot, r * 3 + j] = jnp.broadcast_to(
                    vec[r][:, offset + j : offset + j + 1], (SUB, LANES)
                )

    last, _, first = unit_sweep(first_layer, layers, 0, 0)
    splat(0, last, 0)
    splat(1, first, 0)
    splat(2, first, 32)
    half = 2 * layers
    _, mid, first = unit_sweep(half, 2 * layers, layers, layers)
    splat(3, first, 0)
    splat(4, mid, 16)

    def matrix(slot):
        return [[coef[slot, r * 3 + j] for j in range(3)] for r in range(3)]

    pl.semaphore_wait(
        barrier, 2 + has_below.astype(jnp.int32) + has_above.astype(jnp.int32)
    )

    def remote(slot, src, dst, device):
        return pltpu.make_async_remote_copy(
            src_ref=src,
            dst_ref=dst,
            send_sem=send_sem.at[slot],
            recv_sem=recv_sem.at[slot],
            device_id=device,
            device_id_type=MESH,
        )

    def coefficient(ref, l):
        return ref[mat_ref[l]]

    for stage in range(2):
        slot = 8 * stage
        to_left = remote(
            slot, masked.at[0:2, 1 : layers + 1], halo_hi.at[stage], (depth_id, left)
        )
        to_right = remote(
            slot + 1, masked.at[rows - 2 : rows, 1 : layers + 1], halo_lo.at[stage], (depth_id, right)
        )
        edge_up = remote(slot + 2, masked.at[:, layers], edge_lo.at[stage], (above, plane_id))
        edge_down = remote(slot + 3, masked.at[:, 1], edge_hi.at[stage], (below, plane_id))
        to_left.start()
        to_right.start()

        @pl.when(has_above)
        def _():
            edge_up.start()

        @pl.when(has_below)
        def _():
            edge_down.start()

        def sources(l):
            beta = coefficient(source_ref, l)
            return [beta * field[:, l, c] for c in range(3)]

        def down(l, y):
            t = sub3(sources(l), apply(block_of(low_ref, first_layer + l), y))
            y = apply(block_of(piv_ref, first_layer + l), t)
            for c in range(3):
                sweep[:, l, c] = y[c]
            return tuple(y)

        def up(k, s):
            l = layers - 1 - k
            s = apply(block_of(up_ref, first_layer + l), s)
            return tuple(sweep[:, l, c] - s[c] for c in range(3))

        nothing = tuple(jnp.zeros((rows, SUB, LANES), jnp.float32) for _ in range(3))
        end = lax.fori_loop(0, layers, down, nothing)
        begin = lax.fori_loop(0, layers, up, nothing)

        for c in range(3):
            state_out[0, :, c] = end[c]
            state_out[1, :, c] = begin[c]
            state_out[3, :, c] = nothing[c]
            state_out[4, :, c] = nothing[c]

        def read(ref, index):
            return [ref[index, :, c] for c in range(3)]

        def write(index, value):
            for c in range(3):
                state_out[index, :, c] = value[c]

        is0, is1, is2, is3 = (depth_id == k for k in range(4))
        send_first_up = remote(slot + 4, state_out.at[0], state_in.at[stage, 0], (above, plane_id))
        send_first_down = remote(slot + 4, state_out.at[1], state_in.at[stage, 0], (below, plane_id))
        across_up = remote(slot + 5, state_out.at[2], state_in.at[stage, 1], (above, plane_id))
        across_down = remote(slot + 5, state_out.at[2], state_in.at[stage, 1], (below, plane_id))
        back_down = remote(slot + 6, state_out.at[5], state_in.at[stage, 2], (below, plane_id))
        back_up = remote(slot + 6, state_out.at[5], state_in.at[stage, 2], (above, plane_id))

        @pl.when(is0)
        def _():
            send_first_up.start()

        @pl.when(is3)
        def _():
            send_first_down.start()

        @pl.when(is1)
        def _():
            send_first_up.wait_recv()
            outer = read(state_in.at[stage], 0)
            write(3, outer)
            write(2, add3(read(state_out, 0), apply(matrix(0), outer)))
            across_up.start()

        @pl.when(is2)
        def _():
            send_first_down.wait_recv()
            outer = read(state_in.at[stage], 0)
            inner = add3(outer, apply(matrix(4), read(state_out, 0)))
            write(2, add3(read(state_out, 1), apply(matrix(2), inner)))
            across_down.start()

        if stage == 0:
            flat = (sublane * LANES + lane) * K1
            offset = stream_ref[0] * wrap32(K2) + count_ref[0] * wrap32(K3)

            def noise_layer(l, carry):
                theta = coefficient(theta_ref, l)
                for c in range(3):
                    for x in range(rows):
                        q = c * total_layers + first_layer + l
                        q = q * total_rows + plane_id * rows + x
                        h = flat + ((q * (SUB * LANES)) * K1 + offset)
                        h = h ^ shift_right(h, 16)
                        h = h * K1
                        h = h ^ shift_right(h, 15)
                        h = h * K2
                        h = h ^ shift_right(h, 16)
                        h = (h & 65535).astype(jnp.float32)
                        noise[x, l, c] = theta * (h * (1.0 / 32767.5) - 1.0)
                return carry

            lax.fori_loop(0, layers, noise_layer, 0)

        to_right.wait_recv()
        to_left.wait_recv()

        @pl.when(has_below)
        def _():
            edge_up.wait_recv()
            edge_down.wait_send()
            for c in range(3):
                masked[:, 0, c] = edge_lo[stage, :, c]

        @pl.when(has_above)
        def _():
            edge_down.wait_recv()
            edge_up.wait_send()
            for c in range(3):
                masked[:, layers + 1, c] = edge_hi[stage, :, c]

        @pl.when(jnp.logical_not(has_below))
        def _():
            for c in range(3):
                masked[:, 0, c] = nothing[c]

        @pl.when(jnp.logical_not(has_above))
        def _():
            for c in range(3):
                masked[:, layers + 1, c] = nothing[c]

        def rest_layer(l, carry):
            stiff = coefficient(stiff_ref, l)
            aniso = coefficient(aniso_ref, l)
            for c in range(3):
                lows = [halo_lo[stage, i, l, c] for i in range(2)]
                mine = [masked[x, 1 + l, c] for x in range(rows)]
                highs = [halo_hi[stage, i, l, c] for i in range(2)]
                ext = lows + mine + highs
                for x in range(rows):
                    w = mine[x]
                    prev = pltpu.roll(w, 1, axis=0)
                    after = pltpu.roll(w, SUB - 1, axis=0)
                    near = ext[x + 1] + ext[x + 3]
                    near += pltpu.roll(jnp.where(lane == LANES - 1, prev, w), 1, axis=1)
                    near += pltpu.roll(jnp.where(lane == 0, after, w), LANES - 1, axis=1)
                    far = ext[x] + ext[x + 4]
                    far += pltpu.roll(jnp.where(lane >= LANES - 2, prev, w), 2, axis=1)
                    far += pltpu.roll(jnp.where(lane < 2, after, w), LANES - 2, axis=1)
                    planar = (4.0 / 3.0) * near - (1.0 / 12.0) * far
                    vertical = masked[x, 2 + l, c] + masked[x, l, c]
                    h = stiff * (planar + 0.5 * vertical) + noise[x, l, c]
                    if c == 2:
                        h += aniso * field[x, l, c]
                    rest[x, l, c] = h
            return carry

        lax.fori_loop(0, layers, rest_layer, 0)

        @pl.when(is1)
        def _():
            across_down.wait_recv()
            outer_s = add3(read(state_in.at[stage], 1), apply(matrix(3), read(state_out, 2)))
            write(4, outer_s)
            first_s = add3(read(state_out, 1), apply(matrix(1), read(state_out, 3)))
            write(5, add3(first_s, apply(matrix(2), outer_s)))
            back_down.start()

        @pl.when(is2)
        def _():
            across_up.wait_recv()
            inflow = read(state_in.at[stage], 1)
            write(3, inflow)
            end_y = add3(read(state_out, 0), apply(matrix(0), inflow))
            write(5, end_y)
            back_up.start()
            write(4, add3(read(state_in.at[stage], 0), apply(matrix(4), end_y)))

        @pl.when(is0)
        def _():
            back_down.wait_recv()
            write(4, read(state_in.at[stage], 2))

        @pl.when(is3)
        def _():
            back_up.wait_recv()
            write(3, read(state_in.at[stage], 2))

        lax.fori_loop(0, layers, down, tuple(read(state_out, 3)))

        to_left.wait_send()
        to_right.wait_send()

        def finish_layer(k, s):
            l = layers - 1 - k
            s = apply(block_of(up_ref, first_layer + l), s)
            s = [sweep[:, l, c] - s[c] for c in range(3)]
            alpha = coefficient(damp_ref, l)
            damp = jnp.full((SUB, LANES), alpha, jnp.float32)
            scale = -1.0 / (1.0 + damp * damp)
            for x in range(rows):
                v = [field[x, l, c] for c in range(3)]
                h = [rest[x, l, c] + 0.5 * s[c][x] for c in range(3)]
                torque = cross(v, h)
                twice = cross(v, torque)
                factor = scale * maskf[x]
                change = [(torque[c] + alpha * twice[c]) * factor for c in range(3)]
                start = [base[x, l, c] for c in range(3)]
                if stage == 0:
                    moved = [start[c] + 0.03 * change[c] for c in range(3)]
                else:
                    moved = [start[c] + 0.015 * change[c] for c in range(3)]
                norm = moved[0] * moved[0] + moved[1] * moved[1] + moved[2] * moved[2]
                inverse = lax.rsqrt(norm)
                for c in range(3):
                    if stage == 0:
                        value = moved[c] * inverse
                        field[x, l, c] = value
                        masked[x, 1 + l, c] = value * maskf[x]
                        base[x, l, c] = start[c] + 0.015 * change[c]
                    else:
                        next_ref[c, l, pl.ds(x, SUB, stride=rows), :] = moved[c] * inverse
                        accum_ref[c, l, pl.ds(x, SUB, stride=rows), :] = s[c][x]
            return tuple(s)

        lax.fori_loop(0, layers, finish_layer, tuple(read(state_out, 4)))

        @pl.when(is0)
        def _():
            send_first_up.wait_send()

        @pl.when(is3)
        def _():
            send_first_down.wait_send()

        @pl.when(is1)
        def _():
            across_up.wait_send()
            back_down.wait_send()

        @pl.when(is2)
        def _():
            across_down.wait_send()
            back_up.wait_send()


def local(magnet, mask, *small):
    layers, rows, width = magnet.shape[1:]
    tiles = width // LANES

    def split(a):
        lead = a.shape[:-2]
        a = a.reshape(*lead, rows, tiles, LANES)
        return jnp.swapaxes(a, -3, -2).reshape(*lead, rows * tiles, LANES)

    def join(a):
        lead = a.shape[:-2]
        a = a.reshape(*lead, tiles, rows, LANES)
        return jnp.swapaxes(a, -3, -2).reshape(*lead, rows, width)

    small = list(small)
    for i in (6, 7, 8):
        small[i] = jnp.transpose(small[i], (1, 2, 0))
    vmem = pl.BlockSpec(memory_space=pltpu.VMEM)
    smem = pl.BlockSpec(memory_space=pltpu.SMEM)
    shape = jax.ShapeDtypeStruct((3, layers, rows * tiles, LANES), jnp.float32)
    f32 = jnp.float32
    full = (rows, layers, 3, SUB, LANES)
    state = (rows, 3, SUB, LANES)
    outs = pl.pallas_call(
        functools.partial(kernel, layers, rows),
        out_shape=(shape, shape),
        in_specs=[vmem, vmem] + [smem] * len(small),
        out_specs=(vmem, vmem),
        scratch_shapes=[
            pltpu.VMEM(full, f32),
            pltpu.VMEM(full, f32),
            pltpu.VMEM((rows, layers + 2, 3, SUB, LANES), f32),
            pltpu.VMEM(full, f32),
            pltpu.VMEM(full, f32),
            pltpu.VMEM(full, f32),
            pltpu.VMEM((rows, SUB, LANES), f32),
            pltpu.VMEM((5, 9, SUB, LANES), f32),
            pltpu.VMEM((2 * layers, 3, SUB, LANES), f32),
            pltpu.VMEM((2, 2, layers, 3, SUB, LANES), f32),
            pltpu.VMEM((2, 2, layers, 3, SUB, LANES), f32),
            pltpu.VMEM((2, *state), f32),
            pltpu.VMEM((2, *state), f32),
            pltpu.VMEM((6, *state), f32),
            pltpu.VMEM((2, 3, *state), f32),
            pltpu.SemaphoreType.DMA((16,)),
            pltpu.SemaphoreType.DMA((16,)),
        ],
        compiler_params=pltpu.CompilerParams(
            collective_id=0, has_side_effects=True, vmem_limit_bytes=32 << 20
        ),
    )(split(magnet), split(mask), *small)
    return tuple(join(a) for a in outs)


def solution(mesh):
    placed = (P(None, "depth", "plane", None), P("plane", None), P("depth")) + (P(),) * 10
    out = P(None, "depth", "plane", None)
    return jax.shard_map(
        local, mesh=mesh, in_specs=placed, out_specs=(out, out), check_vma=False
    )
```

```python
import functools

import jax
import jax.numpy as jnp
from jax import lax
from jax.experimental import pallas as pl
from jax.experimental.pallas import tpu as pltpu
from jax.sharding import PartitionSpec as P

MESH = pl.DeviceIdType.MESH
LANES = 128
SUB = 8
K1 = 739982445
K2 = 695872825
K3 = 1597334677


def cross(a, b):
    return [a[1] * b[2] - a[2] * b[1], a[2] * b[0] - a[0] * b[2], a[0] * b[1] - a[1] * b[0]]


def apply(block, vec):
    return [block[r][0] * vec[0] + block[r][1] * vec[1] + block[r][2] * vec[2] for r in range(3)]


def sub3(a, b):
    return [a[c] - b[c] for c in range(3)]


def add3(a, b):
    return [a[c] + b[c] for c in range(3)]


def shift_right(value, amount):
    return lax.shift_right_logical(value, jnp.full(value.shape, amount, jnp.int32))


def kernel(
    layers,
    rows,
    magnet_hbm,
    mask_hbm,
    mat_hbm,
    stiff_hbm,
    aniso_hbm,
    damp_hbm,
    source_hbm,
    theta_hbm,
    piv_hbm,
    low_hbm,
    up_hbm,
    offset_ref,
    next_ref,
    accum_ref,
    magnet_ref,
    mask_ref,
    mat_ref,
    stiff_ref,
    aniso_ref,
    damp_ref,
    source_ref,
    theta_ref,
    piv_ref,
    low_ref,
    up_ref,
    base,
    field,
    masked,
    noise,
    rest,
    sweep,
    maskf,
    coef,
    unit_y,
    halo_lo,
    halo_hi,
    edge_lo,
    edge_hi,
    state_out,
    state_in,
    relay_in,
    load_sem,
    send_sem,
    recv_sem,
    ready_sem,
):
    depth_id = lax.axis_index("depth")
    plane_id = lax.axis_index("plane")
    depth_count = lax.axis_size("depth")
    plane_count = lax.axis_size("plane")
    total_layers = layers * depth_count
    total_rows = rows * plane_count
    left = lax.rem(plane_id + plane_count - 1, plane_count)
    right = lax.rem(plane_id + 1, plane_count)
    above = depth_id + 1
    below = depth_id - 1
    has_below = depth_id > 0
    has_above = depth_id < depth_count - 1
    first_layer = depth_id * layers

    is0, is1, is2, is3 = (depth_id == k for k in range(4))
    mate = depth_id + 1 - 2 * lax.rem(depth_id, 2)
    half_run = 16 if plane_count % 32 == 0 else 1
    relay = plane_id + half_run - 2 * half_run * lax.rem(plane_id // half_run, 2)

    barrier = pltpu.get_barrier_semaphore()

    def greet(device):
        pl.semaphore_signal(barrier, inc=1, device_id=device, device_id_type=MESH)

    @pl.when(is1)
    def _():
        greet((2, plane_id))
        greet((2, relay))
        greet((1, relay))

    greet((mate, plane_id))
    greet((depth_id, left))
    greet((depth_id, right))
    expected = 3 + is1.astype(jnp.int32) + 2 * is2.astype(jnp.int32)

    small_hbm = (
        mat_hbm, stiff_hbm, aniso_hbm, damp_hbm, source_hbm, theta_hbm,
        piv_hbm, low_hbm, up_hbm,
    )
    small_refs = (
        mat_ref, stiff_ref, aniso_ref, damp_ref, source_ref, theta_ref,
        piv_ref, low_ref, up_ref,
    )
    loads = [
        pltpu.make_async_copy(magnet_hbm, magnet_ref, load_sem.at[0]),
        pltpu.make_async_copy(mask_hbm, mask_ref, load_sem.at[1]),
    ]
    for i, (src, dst) in enumerate(zip(small_hbm, small_refs)):
        loads.append(pltpu.make_async_copy(src, dst, load_sem.at[2 + i]))
    for copy in loads:
        copy.start()

    lane = lax.broadcasted_iota(jnp.int32, (SUB, LANES), 1)
    sublane = lax.broadcasted_iota(jnp.int32, (SUB, LANES), 0)

    def block_of(ref, layer):
        return [[ref[i, j, layer] for j in range(3)] for i in range(3)]

    for copy in loads:
        copy.wait()
    for x in range(rows):
        maskf[x] = mask_ref[pl.ds(x, SUB, stride=rows), :].astype(jnp.float32)

    def load_layer(l, carry):
        for c in range(3):
            for x in range(rows):
                value = magnet_ref[c, l, pl.ds(x, SUB, stride=rows), :]
                base[x, l, c] = value
                field[x, l, c] = value
                masked[0, x, 1 + l, c] = value * maskf[x]
        return carry

    lax.fori_loop(0, layers, load_layer, 0)

    def unit(offset, c):
        return (lane == offset + c).astype(jnp.float32)

    zeros = jnp.zeros((SUB, LANES), jnp.float32)

    def unit_sweep(start, count, inject, finish):
        def down(i, y):
            y = [
                jnp.where(lane // 16 == 1, jnp.where(i == inject, unit(16, c), y[c]), y[c])
                for c in range(3)
            ]
            y = apply(block_of(piv_ref, start + i), apply(block_of(low_ref, start + i), y))
            y = [-y[c] for c in range(3)]
            for c in range(3):
                unit_y[i, c] = y[c]
            return tuple(y)

        last = lax.fori_loop(0, count, down, tuple(unit(0, c) for c in range(3)))

        def up(k, s):
            i = count - 1 - k
            s = apply(block_of(up_ref, start + i), s)
            return tuple(unit_y[i, c] - s[c] for c in range(3))

        mid = lax.fori_loop(0, count - finish, up, tuple(unit(32, c) for c in range(3)))
        first = lax.fori_loop(count - finish, count, up, mid)
        return last, mid, first

    def splat(slot, vec, offset):
        for r in range(3):
            for j in range(3):
                coef[slot, r * 3 + j] = jnp.broadcast_to(
                    vec[r][:, offset + j : offset + j + 1], (SUB, LANES)
                )

    def matrix(slot):
        return [[coef[slot, r * 3 + j] for j in range(3)] for r in range(3)]

    def unit_matrices():
        last, _, first = unit_sweep(first_layer, layers, 0, 0)
        splat(0, last, 0)
        splat(1, first, 0)
        splat(2, first, 32)
        _, mid, first = unit_sweep(2 * layers, 2 * layers, layers, layers)
        splat(3, first, 0)
        splat(4, mid, 16)

    def remote(slot, src, dst, device, out_slot=None):
        return pltpu.make_async_remote_copy(
            src_ref=src,
            dst_ref=dst,
            send_sem=send_sem.at[slot if out_slot is None else out_slot],
            recv_sem=recv_sem.at[slot],
            device_id=device,
            device_id_type=MESH,
        )

    def coefficient(ref, l):
        return ref[mat_ref[l]]

    nothing = tuple(jnp.zeros((rows, SUB, LANES), jnp.float32) for _ in range(3))
    for stage in range(2):
        for c in range(3):
            masked[stage, :, 0, c] = nothing[c]
            masked[stage, :, layers + 1, c] = nothing[c]

    for stage in range(2):
        slot = 8 * stage
        to_left = remote(
            slot, masked.at[stage, 0:2, 1 : layers + 1], halo_hi.at[stage], (depth_id, left)
        )
        to_right = remote(
            slot + 1,
            masked.at[stage, rows - 2 : rows, 1 : layers + 1],
            halo_lo.at[stage],
            (depth_id, right),
        )
        top = masked.at[stage, :, layers]
        edge_up = remote(slot + 2, top, edge_lo.at[stage], (above, plane_id))
        edge_down = remote(
            slot + 3, masked.at[stage, :, 1], edge_hi.at[stage], (below, plane_id)
        )
        mine_out = state_out.at[stage]
        mine_in = state_in.at[stage]
        send_first_up = remote(slot + 4, mine_out.at[0], mine_in.at[0], (above, plane_id))
        send_first_down = remote(slot + 4, mine_out.at[1], mine_in.at[0], (below, plane_id))
        across_up = remote(slot + 5, mine_out.at[2], mine_in.at[1], (above, plane_id))
        across_down = remote(slot + 5, mine_out.at[2], mine_in.at[1], (below, plane_id))
        back_down = remote(slot + 6, mine_out.at[5], mine_in.at[2], (below, plane_id))
        back_up = remote(slot + 6, mine_out.at[5], mine_in.at[2], (above, plane_id))
        hop_edge = remote(16, top, relay_in.at[0], (1, relay))
        hop_state = remote(17, mine_out.at[2], relay_in.at[1], (1, relay))
        pass_edge = remote(2, relay_in.at[0], edge_lo.at[0], (2, relay), 18)
        pass_state = remote(5, relay_in.at[1], state_in.at[0, 1], (2, relay), 19)

        def start_edges():
            @pl.when(has_below)
            def _():
                edge_down.start()

            @pl.when(jnp.logical_or(is0, is2))
            def _():
                edge_up.start()

            @pl.when(is1)
            def _():
                if stage == 0:
                    hop_edge.start()
                else:
                    edge_up.start()

        def sources(l):
            beta = coefficient(source_ref, l)
            return [beta * field[:, l, c] for c in range(3)]

        def down(l, y):
            t = sub3(sources(l), apply(block_of(low_ref, first_layer + l), y))
            y = apply(block_of(piv_ref, first_layer + l), t)
            for c in range(3):
                sweep[:, l, c] = y[c]
            return tuple(y)

        def up(k, s):
            l = layers - 1 - k
            s = apply(block_of(up_ref, first_layer + l), s)
            return tuple(sweep[:, l, c] - s[c] for c in range(3))

        def read(ref, index):
            return [ref[index, :, c] for c in range(3)]

        def write(index, value):
            for c in range(3):
                mine_out[index, :, c] = value[c]

        if stage == 1:
            start_edges()
            to_left.start()
            to_right.start()
        end = lax.fori_loop(0, layers, down, nothing)
        write(0, end)
        if stage == 0:
            pl.semaphore_wait(barrier, expected)

            @pl.when(is2)
            def _():
                for i, other in enumerate((plane_id, relay)):
                    pl.semaphore_signal(
                        ready_sem.at[i], inc=1, device_id=(1, other), device_id_type=MESH
                    )

        @pl.when(is0)
        def _():
            send_first_up.start()

        if stage == 0:
            start_edges()
            to_left.start()
            to_right.start()
        begin = lax.fori_loop(0, layers, up, nothing)
        write(1, begin)

        @pl.when(is3)
        def _():
            send_first_down.start()

        write(3, nothing)
        write(4, nothing)
        if stage == 0:
            unit_matrices()

        @pl.when(is1)
        def _():
            send_first_up.wait_recv()
            outer = read(mine_in, 0)
            write(3, outer)
            write(2, add3(read(mine_out, 0), apply(matrix(0), outer)))
            if stage == 0:
                hop_state.start()
            else:
                across_up.start()

        @pl.when(is2)
        def _():
            send_first_down.wait_recv()
            outer = read(mine_in, 0)
            inner_s = add3(outer, apply(matrix(4), read(mine_out, 0)))
            write(2, add3(read(mine_out, 1), apply(matrix(2), inner_s)))
            across_down.start()

        if stage == 0:
            flat = (sublane * LANES + lane) * K1
            offset = offset_ref[0]

            def noise_layer(l, carry):
                theta = coefficient(theta_ref, l)
                for c in range(3):
                    for x in range(rows):
                        q = c * total_layers + first_layer + l
                        q = q * total_rows + plane_id * rows + x
                        h = flat + ((q * (SUB * LANES)) * K1 + offset)
                        h = h ^ shift_right(h, 16)
                        h = h * K1
                        h = h ^ shift_right(h, 15)
                        h = h * K2
                        h = h ^ shift_right(h, 16)
                        h = (h & 65535).astype(jnp.float32)
                        noise[x, l, c] = theta * (h * (1.0 / 32767.5) - 1.0)
                return carry

            lax.fori_loop(0, layers, noise_layer, 0)

            @pl.when(is1)
            def _():
                hop_edge.wait_recv()
                pl.semaphore_wait(ready_sem.at[1], 1)
                pass_edge.start()
                hop_state.wait_recv()
                pass_state.start()

        to_right.wait_recv()
        to_left.wait_recv()

        def rest_layer(l, carry):
            stiff = coefficient(stiff_ref, l)
            aniso = coefficient(aniso_ref, l)
            for c in range(3):
                lows = [halo_lo[stage, i, l, c] for i in range(2)]
                mine = [masked[stage, x, 1 + l, c] for x in range(rows)]
                highs = [halo_hi[stage, i, l, c] for i in range(2)]
                ext = lows + mine + highs
                for x in range(rows):
                    w = mine[x]
                    prev = pltpu.roll(w, 1, axis=0)
                    after = pltpu.roll(w, SUB - 1, axis=0)
                    near = ext[x + 1] + ext[x + 3]
                    near += pltpu.roll(jnp.where(lane == LANES - 1, prev, w), 1, axis=1)
                    near += pltpu.roll(jnp.where(lane == 0, after, w), LANES - 1, axis=1)
                    far = ext[x] + ext[x + 4]
                    far += pltpu.roll(jnp.where(lane >= LANES - 2, prev, w), 2, axis=1)
                    far += pltpu.roll(jnp.where(lane < 2, after, w), LANES - 2, axis=1)
                    planar = (4.0 / 3.0) * near - (1.0 / 12.0) * far
                    vertical = masked[stage, x, 2 + l, c] + masked[stage, x, l, c]
                    h = stiff * (planar + 0.5 * vertical) + noise[x, l, c]
                    if c == 2:
                        h += aniso * field[x, l, c]
                    rest[x, l, c] = h
            return carry

        lax.fori_loop(0, layers, rest_layer, 0)

        @pl.when(has_below)
        def _():
            edge_up.wait_recv()
            half_stiff = 0.5 * coefficient(stiff_ref, 0)
            for c in range(3):
                rest[:, 0, c] += half_stiff * edge_lo[stage, :, c]

        @pl.when(has_above)
        def _():
            edge_down.wait_recv()
            half_stiff = 0.5 * coefficient(stiff_ref, layers - 1)
            for c in range(3):
                rest[:, layers - 1, c] += half_stiff * edge_hi[stage, :, c]

        @pl.when(is1)
        def _():
            across_down.wait_recv()
            outer_s = add3(read(mine_in, 1), apply(matrix(3), read(mine_out, 2)))
            write(4, outer_s)
            first_s = add3(read(mine_out, 1), apply(matrix(1), read(mine_out, 3)))
            write(5, add3(first_s, apply(matrix(2), outer_s)))
            back_down.start()

        @pl.when(is2)
        def _():
            across_up.wait_recv()
            inflow = read(mine_in, 1)
            write(3, inflow)
            end_y = add3(read(mine_out, 0), apply(matrix(0), inflow))
            write(5, end_y)
            back_up.start()
            write(4, add3(read(mine_in, 0), apply(matrix(4), end_y)))

        @pl.when(is0)
        def _():
            back_down.wait_recv()
            write(4, read(mine_in, 2))

        @pl.when(is3)
        def _():
            back_up.wait_recv()
            write(3, read(mine_in, 2))

        lax.fori_loop(0, layers, down, tuple(read(mine_out, 3)))

        def finish_layer(k, s):
            l = layers - 1 - k
            s = apply(block_of(up_ref, first_layer + l), s)
            s = [sweep[:, l, c] - s[c] for c in range(3)]
            alpha = coefficient(damp_ref, l)
            damp = jnp.full((SUB, LANES), alpha, jnp.float32)
            scale = -1.0 / (1.0 + damp * damp)
            for x in range(rows):
                v = [field[x, l, c] for c in range(3)]
                h = [rest[x, l, c] + 0.5 * s[c][x] for c in range(3)]
                torque = cross(v, h)
                twice = cross(v, torque)
                factor = scale * maskf[x]
                change = [(torque[c] + alpha * twice[c]) * factor for c in range(3)]
                start = [base[x, l, c] for c in range(3)]
                if stage == 0:
                    moved = [start[c] + 0.03 * change[c] for c in range(3)]
                else:
                    moved = [start[c] + 0.015 * change[c] for c in range(3)]
                norm = moved[0] * moved[0] + moved[1] * moved[1] + moved[2] * moved[2]
                inverse = lax.rsqrt(norm)
                for c in range(3):
                    if stage == 0:
                        value = moved[c] * inverse
                        field[x, l, c] = value
                        masked[1, x, 1 + l, c] = value * maskf[x]
                        base[x, l, c] = start[c] + 0.015 * change[c]
                    else:
                        next_ref[c, l, pl.ds(x, SUB, stride=rows), :] = moved[c] * inverse
                        accum_ref[c, l, pl.ds(x, SUB, stride=rows), :] = s[c][x]
            return tuple(s)

        lax.fori_loop(0, layers, finish_layer, tuple(read(mine_out, 4)))
        if stage == 0:

            @pl.when(is1)
            def _():
                pl.semaphore_wait(ready_sem.at[0], 1)

        if stage == 1:
            drains.append((to_left, to_right, edge_up, edge_down))
        else:
            drains = [(to_left, to_right, edge_up, edge_down)]
        ends = [send_first_up, send_first_down, across_up, across_down, back_down, back_up]
        drains[-1] = drains[-1] + tuple(ends) + (hop_edge, hop_state, pass_edge, pass_state)

    for stage, copies in enumerate(drains):
        (to_left, to_right, edge_up, edge_down, first_up, first_down, across_up, across_down,
         back_down, back_up, hop_edge, hop_state, pass_edge, pass_state) = copies
        to_left.wait_send()
        to_right.wait_send()

        @pl.when(has_below)
        def _():
            edge_down.wait_send()

        @pl.when(jnp.logical_or(is0, is2))
        def _():
            edge_up.wait_send()

        @pl.when(is0)
        def _():
            first_up.wait_send()

        @pl.when(is3)
        def _():
            first_down.wait_send()

        @pl.when(is1)
        def _():
            back_down.wait_send()
            if stage == 0:
                for copy in (hop_edge, hop_state, pass_edge, pass_state):
                    copy.wait_send()
            else:
                edge_up.wait_send()
                across_up.wait_send()

        @pl.when(is2)
        def _():
            across_down.wait_send()
            back_up.wait_send()


def local(magnet, mask, *small):
    layers, rows, width = magnet.shape[1:]
    tiles = width // LANES

    def split(a):
        lead = a.shape[:-2]
        a = a.reshape(*lead, rows, tiles, LANES)
        return jnp.swapaxes(a, -3, -2).reshape(*lead, rows * tiles, LANES)

    def join(a):
        lead = a.shape[:-2]
        a = a.reshape(*lead, tiles, rows, LANES)
        return jnp.swapaxes(a, -3, -2).reshape(*lead, rows, width)

    small = list(small)
    for i in (6, 7, 8):
        small[i] = jnp.transpose(small[i], (1, 2, 0))
    vmem = pl.BlockSpec(memory_space=pltpu.VMEM)
    hbm = pl.BlockSpec(memory_space=pltpu.MemorySpace.HBM)
    offset = small[9] * K2 + small[10] * K3
    operands = [split(magnet), split(mask), *small[:9]]
    operands = [pltpu.with_memory_space_constraint(a, pltpu.MemorySpace.HBM) for a in operands]
    held = [pltpu.VMEM(a.shape, a.dtype) for a in operands[:2]]
    held += [pltpu.SMEM(a.shape, a.dtype) for a in operands[2:]]
    shape = jax.ShapeDtypeStruct((3, layers, rows * tiles, LANES), jnp.float32)
    f32 = jnp.float32
    full = (rows, layers, 3, SUB, LANES)
    state = (rows, 3, SUB, LANES)
    outs = pl.pallas_call(
        functools.partial(kernel, layers, rows),
        out_shape=(shape, shape),
        in_specs=[hbm] * len(operands) + [pl.BlockSpec(memory_space=pltpu.SMEM)],
        out_specs=(vmem, vmem),
        scratch_shapes=held + [
            pltpu.VMEM(full, f32),
            pltpu.VMEM(full, f32),
            pltpu.VMEM((2, rows, layers + 2, 3, SUB, LANES), f32),
            pltpu.VMEM(full, f32),
            pltpu.VMEM(full, f32),
            pltpu.VMEM(full, f32),
            pltpu.VMEM((rows, SUB, LANES), f32),
            pltpu.VMEM((5, 9, SUB, LANES), f32),
            pltpu.VMEM((2 * layers, 3, SUB, LANES), f32),
            pltpu.VMEM((2, 2, layers, 3, SUB, LANES), f32),
            pltpu.VMEM((2, 2, layers, 3, SUB, LANES), f32),
            pltpu.VMEM((2, *state), f32),
            pltpu.VMEM((2, *state), f32),
            pltpu.VMEM((2, 6, *state), f32),
            pltpu.VMEM((2, 3, *state), f32),
            pltpu.VMEM((2, *state), f32),
            pltpu.SemaphoreType.DMA((len(operands),)),
            pltpu.SemaphoreType.DMA((20,)),
            pltpu.SemaphoreType.DMA((20,)),
            pltpu.SemaphoreType.REGULAR((2,)),
        ],
        compiler_params=pltpu.CompilerParams(
            collective_id=0, has_side_effects=True, vmem_limit_bytes=32 << 20
        ),
    )(*operands, offset)
    return tuple(join(a) for a in outs)


def solution(mesh):
    placed = (P(None, "depth", "plane", None), P("plane", None), P("depth")) + (P(),) * 10
    out = P(None, "depth", "plane", None)
    return jax.shard_map(
        local, mesh=mesh, in_specs=placed, out_specs=(out, out), check_vma=False
    )
```

```python
import functools

import jax
import jax.numpy as jnp
from jax import lax
from jax.experimental import pallas as pl
from jax.experimental.pallas import tpu as pltpu
from jax.sharding import PartitionSpec as P

MESH = pl.DeviceIdType.MESH
LANES = 128
SUB = 8
K1 = 739982445
K2 = 695872825
K3 = 1597334677


def cross(a, b):
    return [a[1] * b[2] - a[2] * b[1], a[2] * b[0] - a[0] * b[2], a[0] * b[1] - a[1] * b[0]]


def apply(block, vec):
    return [block[r][0] * vec[0] + block[r][1] * vec[1] + block[r][2] * vec[2] for r in range(3)]


def sub3(a, b):
    return [a[c] - b[c] for c in range(3)]


def add3(a, b):
    return [a[c] + b[c] for c in range(3)]


def shift_right(value, amount):
    return lax.shift_right_logical(value, jnp.full(value.shape, amount, jnp.int32))


def kernel(
    layers,
    rows,
    magnet_hbm,
    mask_hbm,
    mat_hbm,
    stiff_hbm,
    aniso_hbm,
    damp_hbm,
    source_hbm,
    theta_hbm,
    piv_hbm,
    low_hbm,
    up_hbm,
    offset_ref,
    next_ref,
    accum_ref,
    magnet_ref,
    mask_ref,
    mat_ref,
    stiff_ref,
    aniso_ref,
    damp_ref,
    source_ref,
    theta_ref,
    piv_ref,
    low_ref,
    up_ref,
    base,
    field,
    masked,
    noise,
    rest,
    sweep,
    maskf,
    coef,
    unit_y,
    halo_lo,
    halo_hi,
    edge_lo,
    edge_hi,
    state_out,
    state_in,
    relay_in,
    load_sem,
    send_sem,
    recv_sem,
    ready_sem,
):
    depth_id = lax.axis_index("depth")
    plane_id = lax.axis_index("plane")
    depth_count = lax.axis_size("depth")
    plane_count = lax.axis_size("plane")
    total_layers = layers * depth_count
    total_rows = rows * plane_count
    left = lax.rem(plane_id + plane_count - 1, plane_count)
    right = lax.rem(plane_id + 1, plane_count)
    above = depth_id + 1
    below = depth_id - 1
    has_below = depth_id > 0
    has_above = depth_id < depth_count - 1
    first_layer = depth_id * layers

    is0, is1, is2, is3 = (depth_id == k for k in range(4))
    mate = depth_id + 1 - 2 * lax.rem(depth_id, 2)
    half_run = 16 if plane_count % 32 == 0 else plane_count // 2
    run = 2 * half_run
    place = lax.rem(plane_id, run)
    relay = plane_id + half_run - 2 * half_run * (place // half_run)
    far = jnp.logical_or(place == 0, place == run - 1)
    upper = depth_id >= 2

    barrier = pltpu.get_barrier_semaphore()

    def greet(device):
        pl.semaphore_signal(barrier, inc=1, device_id=device, device_id_type=MESH)

    @pl.when(is1)
    def _():
        greet((2, plane_id))
        greet((2, relay))
        greet((1, relay))

    greet((mate, plane_id))
    greet((depth_id, left))
    greet((depth_id, right))
    expected = 3 + is1.astype(jnp.int32) + 2 * is2.astype(jnp.int32)

    small_hbm = (
        mat_hbm, stiff_hbm, aniso_hbm, damp_hbm, source_hbm, theta_hbm,
        piv_hbm, low_hbm, up_hbm,
    )
    small_refs = (
        mat_ref, stiff_ref, aniso_ref, damp_ref, source_ref, theta_ref,
        piv_ref, low_ref, up_ref,
    )
    loads = [
        pltpu.make_async_copy(magnet_hbm, magnet_ref, load_sem.at[0]),
        pltpu.make_async_copy(mask_hbm, mask_ref, load_sem.at[1]),
    ]
    for i, (src, dst) in enumerate(zip(small_hbm, small_refs)):
        loads.append(pltpu.make_async_copy(src, dst, load_sem.at[2 + i]))
    for copy in loads:
        copy.start()

    def meet():
        pl.semaphore_wait(barrier, expected)

        @pl.when(is2)
        def _():
            for i, other in enumerate((plane_id, relay)):
                pl.semaphore_signal(
                    ready_sem.at[i], inc=1, device_id=(1, other), device_id_type=MESH
                )

    @pl.when(jnp.logical_not(far))
    def _():
        meet()

    lane = lax.broadcasted_iota(jnp.int32, (SUB, LANES), 1)
    sublane = lax.broadcasted_iota(jnp.int32, (SUB, LANES), 0)

    def block_of(ref, layer):
        return [[ref[i, j, layer] for j in range(3)] for i in range(3)]

    for copy in loads:
        copy.wait()
    for x in range(rows):
        maskf[x] = mask_ref[pl.ds(x, SUB, stride=rows), :].astype(jnp.float32)

    def load_layer(l, carry):
        for c in range(3):
            for x in range(rows):
                value = magnet_ref[c, l, pl.ds(x, SUB, stride=rows), :]
                base[x, l, c] = value
                field[x, l, c] = value
                masked[0, x, 1 + l, c] = value * maskf[x]
        return carry

    lax.fori_loop(0, layers, load_layer, 0)

    def unit(offset, c):
        return (lane == offset + c).astype(jnp.float32)

    zeros = jnp.zeros((SUB, LANES), jnp.float32)

    def unit_sweep(start, count, inject, finish):
        def down(i, y):
            y = [
                jnp.where(lane // 16 == 1, jnp.where(i == inject, unit(16, c), y[c]), y[c])
                for c in range(3)
            ]
            y = apply(block_of(piv_ref, start + i), apply(block_of(low_ref, start + i), y))
            y = [-y[c] for c in range(3)]
            for c in range(3):
                unit_y[i, c] = y[c]
            return tuple(y)

        last = lax.fori_loop(0, count, down, tuple(unit(0, c) for c in range(3)))

        def up(k, s):
            i = count - 1 - k
            s = apply(block_of(up_ref, start + i), s)
            return tuple(unit_y[i, c] - s[c] for c in range(3))

        mid = lax.fori_loop(0, count - finish, up, tuple(unit(32, c) for c in range(3)))
        first = lax.fori_loop(count - finish, count, up, mid)
        return last, mid, first

    def splat(slot, vec, offset):
        for r in range(3):
            for j in range(3):
                coef[slot, r * 3 + j] = jnp.broadcast_to(
                    vec[r][:, offset + j : offset + j + 1], (SUB, LANES)
                )

    def matrix(slot):
        return [[coef[slot, r * 3 + j] for j in range(3)] for r in range(3)]

    def unit_matrices():
        last, _, first = unit_sweep(first_layer, layers, 0, 0)
        splat(0, last, 0)
        splat(1, first, 0)
        splat(2, first, 32)
        _, mid, first = unit_sweep(2 * layers, 2 * layers, layers, layers)
        splat(3, first, 0)
        splat(4, mid, 16)

    def remote(slot, src, dst, device, out_slot=None):
        return pltpu.make_async_remote_copy(
            src_ref=src,
            dst_ref=dst,
            send_sem=send_sem.at[slot if out_slot is None else out_slot],
            recv_sem=recv_sem.at[slot],
            device_id=device,
            device_id_type=MESH,
        )

    def coefficient(ref, l):
        return ref[mat_ref[l]]

    nothing = tuple(jnp.zeros((rows, SUB, LANES), jnp.float32) for _ in range(3))
    for stage in range(2):
        for c in range(3):
            masked[stage, :, 0, c] = nothing[c]
            masked[stage, :, layers + 1, c] = nothing[c]

    for stage in range(2):
        slot = 8 * stage
        to_left = remote(
            slot, masked.at[stage, 0:2, 1 : layers + 1], halo_hi.at[stage], (depth_id, left)
        )
        to_right = remote(
            slot + 1,
            masked.at[stage, rows - 2 : rows, 1 : layers + 1],
            halo_lo.at[stage],
            (depth_id, right),
        )
        top = masked.at[stage, :, layers]
        edge_up = remote(slot + 2, top, edge_lo.at[stage], (above, plane_id))
        edge_down = remote(
            slot + 3, masked.at[stage, :, 1], edge_hi.at[stage], (below, plane_id)
        )
        mine_out = state_out.at[stage]
        mine_in = state_in.at[stage]
        send_first_up = remote(slot + 4, mine_out.at[0], mine_in.at[0], (above, plane_id))
        send_first_down = remote(slot + 4, mine_out.at[1], mine_in.at[0], (below, plane_id))
        across_up = remote(slot + 5, mine_out.at[2], mine_in.at[1], (above, plane_id))
        across_down = remote(slot + 5, mine_out.at[2], mine_in.at[1], (below, plane_id))
        back_down = remote(slot + 6, mine_out.at[5], mine_in.at[2], (below, plane_id))
        back_up = remote(slot + 6, mine_out.at[5], mine_in.at[2], (above, plane_id))
        hop_edge = remote(16, top, relay_in.at[0], (1, relay))
        hop_state = remote(17, mine_out.at[2], relay_in.at[1], (1, relay))
        pass_edge = remote(2, relay_in.at[0], edge_lo.at[0], (2, relay), 18)
        pass_state = remote(5, relay_in.at[1], state_in.at[0, 1], (2, relay), 19)

        def start_edges():
            @pl.when(has_below)
            def _():
                edge_down.start()

            @pl.when(jnp.logical_or(is0, is2))
            def _():
                edge_up.start()

            @pl.when(is1)
            def _():
                if stage == 0:
                    hop_edge.start()
                else:
                    edge_up.start()

        def sources(l):
            beta = coefficient(source_ref, l)
            return [beta * field[:, l, c] for c in range(3)]

        def down(l, y):
            t = sub3(sources(l), apply(block_of(low_ref, first_layer + l), y))
            y = apply(block_of(piv_ref, first_layer + l), t)
            for c in range(3):
                sweep[:, l, c] = y[c]
            return tuple(y)

        def up(k, s):
            l = layers - 1 - k
            s = apply(block_of(up_ref, first_layer + l), s)
            return tuple(sweep[:, l, c] - s[c] for c in range(3))

        def read(ref, index):
            return [ref[index, :, c] for c in range(3)]

        def write(index, value):
            for c in range(3):
                mine_out[index, :, c] = value[c]

        def start_halos():
            to_left.start()
            to_right.start()

        if stage == 1:

            @pl.when(jnp.logical_not(upper))
            def _():
                start_halos()

            start_edges()
        end = lax.fori_loop(0, layers, down, nothing)
        write(0, end)
        if stage == 0:

            @pl.when(far)
            def _():
                meet()

        @pl.when(is0)
        def _():
            send_first_up.start()

        if stage == 0:
            start_halos()
            start_edges()
        begin = lax.fori_loop(0, layers, up, nothing)
        write(1, begin)

        @pl.when(is3)
        def _():
            send_first_down.start()

        write(3, nothing)
        write(4, nothing)
        if stage == 0:
            unit_matrices()

        @pl.when(is1)
        def _():
            send_first_up.wait_recv()
            outer = read(mine_in, 0)
            write(3, outer)
            write(2, add3(read(mine_out, 0), apply(matrix(0), outer)))
            if stage == 0:
                hop_state.start()
            else:
                across_up.start()

        @pl.when(is2)
        def _():
            send_first_down.wait_recv()
            outer = read(mine_in, 0)
            inner_s = add3(outer, apply(matrix(4), read(mine_out, 0)))
            write(2, add3(read(mine_out, 1), apply(matrix(2), inner_s)))
            across_down.start()

        if stage == 0:
            flat = (sublane * LANES + lane) * K1
            offset = offset_ref[0]

            def noise_layer(l, carry):
                theta = coefficient(theta_ref, l)
                for c in range(3):
                    for x in range(rows):
                        q = c * total_layers + first_layer + l
                        q = q * total_rows + plane_id * rows + x
                        h = flat + ((q * (SUB * LANES)) * K1 + offset)
                        h = h ^ shift_right(h, 16)
                        h = h * K1
                        h = h ^ shift_right(h, 15)
                        h = h * K2
                        h = h ^ shift_right(h, 16)
                        h = (h & 65535).astype(jnp.float32)
                        noise[x, l, c] = theta * (h * (1.0 / 32767.5) - 1.0)
                return carry

            lax.fori_loop(0, layers, noise_layer, 0)

            @pl.when(is1)
            def _():
                hop_edge.wait_recv()
                pl.semaphore_wait(ready_sem.at[1], 1)
                pass_edge.start()
                hop_state.wait_recv()
                pass_state.start()

        if stage == 1:

            @pl.when(upper)
            def _():
                start_halos()

        def settle():
            lax.fori_loop(0, layers, down, tuple(read(mine_out, 3)))

        def rest_layer(l, carry):
            stiff = coefficient(stiff_ref, l)
            aniso = coefficient(aniso_ref, l)
            for c in range(3):
                mine = [masked[stage, x, 1 + l, c] for x in range(rows)]
                for x in range(rows):
                    w = mine[x]
                    prev = pltpu.roll(w, 1, axis=0)
                    after = pltpu.roll(w, SUB - 1, axis=0)
                    near = pltpu.roll(jnp.where(lane == LANES - 1, prev, w), 1, axis=1)
                    near += pltpu.roll(jnp.where(lane == 0, after, w), LANES - 1, axis=1)
                    far_sum = pltpu.roll(jnp.where(lane >= LANES - 2, prev, w), 2, axis=1)
                    far_sum += pltpu.roll(jnp.where(lane < 2, after, w), LANES - 2, axis=1)
                    for other in range(rows):
                        if abs(other - x) == 1:
                            near += mine[other]
                        elif abs(other - x) == 2:
                            far_sum += mine[other]
                    planar = (4.0 / 3.0) * near - (1.0 / 12.0) * far_sum
                    vertical = masked[stage, x, 2 + l, c] + masked[stage, x, l, c]
                    h = stiff * (planar + 0.5 * vertical) + noise[x, l, c]
                    if c == 2:
                        h += aniso * field[x, l, c]
                    rest[x, l, c] = h
            return carry

        lax.fori_loop(0, layers, rest_layer, 0)

        @pl.when(is2)
        def _():
            across_up.wait_recv()
            inflow = read(mine_in, 1)
            write(3, inflow)
            end_y = add3(read(mine_out, 0), apply(matrix(0), inflow))
            write(5, end_y)
            back_up.start()
            write(4, add3(read(mine_in, 0), apply(matrix(4), end_y)))
            settle()

        @pl.when(is3)
        def _():
            back_up.wait_recv()
            write(3, read(mine_in, 2))
            settle()

        @pl.when(jnp.logical_not(upper))
        def _():
            settle()

        to_right.wait_recv()
        to_left.wait_recv()

        def halo_layer(l, carry):
            stiff = coefficient(stiff_ref, l)
            one = stiff * (4.0 / 3.0)
            two = stiff * (-1.0 / 12.0)
            for c in range(3):
                lows = [halo_lo[stage, i, l, c] for i in range(2)]
                highs = [halo_hi[stage, i, l, c] for i in range(2)]
                rest[0, l, c] += one * lows[1] + two * lows[0]
                rest[1, l, c] += two * lows[1]
                rest[rows - 1, l, c] += one * highs[0] + two * highs[1]
                rest[rows - 2, l, c] += two * highs[0]
            return carry

        lax.fori_loop(0, layers, halo_layer, 0)

        @pl.when(has_below)
        def _():
            edge_up.wait_recv()
            half_stiff = 0.5 * coefficient(stiff_ref, 0)
            for c in range(3):
                rest[:, 0, c] += half_stiff * edge_lo[stage, :, c]

        @pl.when(has_above)
        def _():
            edge_down.wait_recv()
            half_stiff = 0.5 * coefficient(stiff_ref, layers - 1)
            for c in range(3):
                rest[:, layers - 1, c] += half_stiff * edge_hi[stage, :, c]

        @pl.when(is1)
        def _():
            across_down.wait_recv()
            outer_s = add3(read(mine_in, 1), apply(matrix(3), read(mine_out, 2)))
            write(4, outer_s)
            first_s = add3(read(mine_out, 1), apply(matrix(1), read(mine_out, 3)))
            write(5, add3(first_s, apply(matrix(2), outer_s)))
            back_down.start()

        @pl.when(is0)
        def _():
            back_down.wait_recv()
            write(4, read(mine_in, 2))

        def finish_layer(k, s):
            l = layers - 1 - k
            s = apply(block_of(up_ref, first_layer + l), s)
            s = [sweep[:, l, c] - s[c] for c in range(3)]
            alpha = coefficient(damp_ref, l)
            damp = jnp.full((SUB, LANES), alpha, jnp.float32)
            scale = -1.0 / (1.0 + damp * damp)
            for x in range(rows):
                v = [field[x, l, c] for c in range(3)]
                h = [rest[x, l, c] + 0.5 * s[c][x] for c in range(3)]
                torque = cross(v, h)
                twice = cross(v, torque)
                factor = scale * maskf[x]
                change = [(torque[c] + alpha * twice[c]) * factor for c in range(3)]
                start = [base[x, l, c] for c in range(3)]
                if stage == 0:
                    moved = [start[c] + 0.03 * change[c] for c in range(3)]
                else:
                    moved = [start[c] + 0.015 * change[c] for c in range(3)]
                norm = moved[0] * moved[0] + moved[1] * moved[1] + moved[2] * moved[2]
                inverse = lax.rsqrt(norm)
                for c in range(3):
                    if stage == 0:
                        value = moved[c] * inverse
                        field[x, l, c] = value
                        masked[1, x, 1 + l, c] = value * maskf[x]
                        base[x, l, c] = start[c] + 0.015 * change[c]
                    else:
                        next_ref[c, l, pl.ds(x, SUB, stride=rows), :] = moved[c] * inverse
                        accum_ref[c, l, pl.ds(x, SUB, stride=rows), :] = s[c][x]
            return tuple(s)

        lax.fori_loop(0, layers, finish_layer, tuple(read(mine_out, 4)))
        if stage == 0:

            @pl.when(is1)
            def _():
                pl.semaphore_wait(ready_sem.at[0], 1)

        if stage == 1:
            drains.append((to_left, to_right, edge_up, edge_down))
        else:
            drains = [(to_left, to_right, edge_up, edge_down)]
        ends = [send_first_up, send_first_down, across_up, across_down, back_down, back_up]
        drains[-1] = drains[-1] + tuple(ends) + (hop_edge, hop_state, pass_edge, pass_state)

    for stage, copies in enumerate(drains):
        (to_left, to_right, edge_up, edge_down, first_up, first_down, across_up, across_down,
         back_down, back_up, hop_edge, hop_state, pass_edge, pass_state) = copies
        to_left.wait_send()
        to_right.wait_send()

        @pl.when(has_below)
        def _():
            edge_down.wait_send()

        @pl.when(jnp.logical_or(is0, is2))
        def _():
            edge_up.wait_send()

        @pl.when(is0)
        def _():
            first_up.wait_send()

        @pl.when(is3)
        def _():
            first_down.wait_send()

        @pl.when(is1)
        def _():
            back_down.wait_send()
            if stage == 0:
                for copy in (hop_edge, hop_state, pass_edge, pass_state):
                    copy.wait_send()
            else:
                edge_up.wait_send()
                across_up.wait_send()

        @pl.when(is2)
        def _():
            across_down.wait_send()
            back_up.wait_send()


def local(magnet, mask, *small):
    layers, rows, width = magnet.shape[1:]
    tiles = width // LANES

    def split(a):
        lead = a.shape[:-2]
        a = a.reshape(*lead, rows, tiles, LANES)
        return jnp.swapaxes(a, -3, -2).reshape(*lead, rows * tiles, LANES)

    def join(a):
        lead = a.shape[:-2]
        a = a.reshape(*lead, tiles, rows, LANES)
        return jnp.swapaxes(a, -3, -2).reshape(*lead, rows, width)

    small = list(small)
    for i in (6, 7, 8):
        small[i] = jnp.transpose(small[i], (1, 2, 0))
    vmem = pl.BlockSpec(memory_space=pltpu.VMEM)
    hbm = pl.BlockSpec(memory_space=pltpu.MemorySpace.HBM)
    offset = small[9] * K2 + small[10] * K3
    operands = [split(magnet), split(mask), *small[:9]]
    operands = [pltpu.with_memory_space_constraint(a, pltpu.MemorySpace.HBM) for a in operands]
    held = [pltpu.VMEM(a.shape, a.dtype) for a in operands[:2]]
    held += [pltpu.SMEM(a.shape, a.dtype) for a in operands[2:]]
    shape = jax.ShapeDtypeStruct((3, layers, rows * tiles, LANES), jnp.float32)
    f32 = jnp.float32
    full = (rows, layers, 3, SUB, LANES)
    state = (rows, 3, SUB, LANES)
    outs = pl.pallas_call(
        functools.partial(kernel, layers, rows),
        out_shape=(shape, shape),
        in_specs=[hbm] * len(operands) + [pl.BlockSpec(memory_space=pltpu.SMEM)],
        out_specs=(vmem, vmem),
        scratch_shapes=held + [
            pltpu.VMEM(full, f32),
            pltpu.VMEM(full, f32),
            pltpu.VMEM((2, rows, layers + 2, 3, SUB, LANES), f32),
            pltpu.VMEM(full, f32),
            pltpu.VMEM(full, f32),
            pltpu.VMEM(full, f32),
            pltpu.VMEM((rows, SUB, LANES), f32),
            pltpu.VMEM((5, 9, SUB, LANES), f32),
            pltpu.VMEM((2 * layers, 3, SUB, LANES), f32),
            pltpu.VMEM((2, 2, layers, 3, SUB, LANES), f32),
            pltpu.VMEM((2, 2, layers, 3, SUB, LANES), f32),
            pltpu.VMEM((2, *state), f32),
            pltpu.VMEM((2, *state), f32),
            pltpu.VMEM((2, 6, *state), f32),
            pltpu.VMEM((2, 3, *state), f32),
            pltpu.VMEM((2, *state), f32),
            pltpu.SemaphoreType.DMA((len(operands),)),
            pltpu.SemaphoreType.DMA((20,)),
            pltpu.SemaphoreType.DMA((20,)),
            pltpu.SemaphoreType.REGULAR((2,)),
        ],
        compiler_params=pltpu.CompilerParams(
            collective_id=0, has_side_effects=True, vmem_limit_bytes=32 << 20
        ),
    )(*operands, offset)
    return tuple(join(a) for a in outs)


def solution(mesh):
    placed = (P(None, "depth", "plane", None), P("plane", None), P("depth")) + (P(),) * 10
    out = P(None, "depth", "plane", None)
    return jax.shard_map(
        local, mesh=mesh, in_specs=placed, out_specs=(out, out), check_vma=False
    )
```

```python
import functools

import jax
import jax.numpy as jnp
from jax import lax
from jax.experimental import pallas as pl
from jax.experimental.pallas import tpu as pltpu
from jax.sharding import PartitionSpec as P

MESH = pl.DeviceIdType.MESH
LANES = 128
SUB = 8
K1 = 739982445
K2 = 695872825
K3 = 1597334677


def cross(a, b):
    return [a[1] * b[2] - a[2] * b[1], a[2] * b[0] - a[0] * b[2], a[0] * b[1] - a[1] * b[0]]


def apply(block, vec):
    return [block[r][0] * vec[0] + block[r][1] * vec[1] + block[r][2] * vec[2] for r in range(3)]


def sub3(a, b):
    return [a[c] - b[c] for c in range(3)]


def add3(a, b):
    return [a[c] + b[c] for c in range(3)]


def shift_right(value, amount):
    return lax.shift_right_logical(value, jnp.full(value.shape, amount, jnp.int32))


def kernel(
    layers,
    rows,
    magnet_hbm,
    mask_hbm,
    mat_hbm,
    stiff_hbm,
    aniso_hbm,
    damp_hbm,
    source_hbm,
    theta_hbm,
    piv_hbm,
    low_hbm,
    up_hbm,
    stream_ref,
    count_ref,
    next_ref,
    accum_ref,
    magnet_ref,
    mask_ref,
    mat_ref,
    stiff_ref,
    aniso_ref,
    damp_ref,
    source_ref,
    theta_ref,
    piv_ref,
    low_ref,
    up_ref,
    base,
    field,
    masked,
    noise,
    rest,
    sweep,
    maskf,
    coef,
    unit_y,
    halo_lo,
    halo_hi,
    edge_lo,
    edge_hi,
    state_out,
    state_in,
    relay_in,
    load_sem,
    send_sem,
    recv_sem,
    ready_sem,
):
    depth_id = lax.axis_index("depth")
    plane_id = lax.axis_index("plane")
    depth_count = lax.axis_size("depth")
    plane_count = lax.axis_size("plane")
    total_layers = layers * depth_count
    total_rows = rows * plane_count
    left = lax.rem(plane_id + plane_count - 1, plane_count)
    right = lax.rem(plane_id + 1, plane_count)
    above = depth_id + 1
    below = depth_id - 1
    has_below = depth_id > 0
    has_above = depth_id < depth_count - 1
    first_layer = depth_id * layers

    is0, is1, is2, is3 = (depth_id == k for k in range(4))
    mate = depth_id + 1 - 2 * lax.rem(depth_id, 2)
    half_run = 16 if plane_count % 32 == 0 else plane_count // 2
    run = 2 * half_run
    place = lax.rem(plane_id, run)
    relay = plane_id + half_run - 2 * half_run * (place // half_run)
    wrap_left = place == 0
    wrap_right = place == run - 1
    post_place = half_run + (1 if plane_count % 32 == 0 else 0)
    post = jnp.logical_and(depth_id < 2, place == post_place)

    def turn(shift):
        return lax.rem(plane_id + shift + plane_count, plane_count)

    upper = depth_id >= 2

    barrier = pltpu.get_barrier_semaphore()

    def greet(device):
        pl.semaphore_signal(barrier, inc=1, device_id=device, device_id_type=MESH)

    @pl.when(is1)
    def _():
        greet((2, plane_id))
        greet((2, relay))
        greet((1, relay))

    @pl.when(post)
    def _():
        for group in (depth_id, depth_id + 2):
            greet((group, turn(-post_place)))
            greet((group, turn(-post_place - 1)))

    greet((mate, plane_id))

    @pl.when(jnp.logical_not(wrap_left))
    def _():
        greet((depth_id, left))

    @pl.when(jnp.logical_not(wrap_right))
    def _():
        greet((depth_id, right))

    expected = 3 + is1.astype(jnp.int32) + 2 * is2.astype(jnp.int32)

    small_hbm = (
        mat_hbm, stiff_hbm, aniso_hbm, damp_hbm, source_hbm, theta_hbm,
        piv_hbm, low_hbm, up_hbm,
    )
    small_refs = (
        mat_ref, stiff_ref, aniso_ref, damp_ref, source_ref, theta_ref,
        piv_ref, low_ref, up_ref,
    )
    loads = [
        pltpu.make_async_copy(magnet_hbm, magnet_ref, load_sem.at[0]),
        pltpu.make_async_copy(mask_hbm, mask_ref, load_sem.at[1]),
    ]
    for i, (src, dst) in enumerate(zip(small_hbm, small_refs)):
        loads.append(pltpu.make_async_copy(src, dst, load_sem.at[2 + i]))
    for copy in loads:
        copy.start()

    pl.semaphore_wait(barrier, expected)

    def tell(index, device):
        pl.semaphore_signal(ready_sem.at[index], inc=1, device_id=device, device_id_type=MESH)

    @pl.when(is2)
    def _():
        tell(0, (1, plane_id))
        tell(1, (1, relay))

    for high in range(2):

        @pl.when(jnp.logical_and(wrap_left, upper == bool(high)))
        def _():
            tell(2 + 2 * high, (lax.rem(depth_id, 2), turn(post_place)))

        @pl.when(jnp.logical_and(wrap_right, upper == bool(high)))
        def _():
            tell(3 + 2 * high, (lax.rem(depth_id, 2), turn(post_place + 1)))

    lane = lax.broadcasted_iota(jnp.int32, (SUB, LANES), 1)
    sublane = lax.broadcasted_iota(jnp.int32, (SUB, LANES), 0)

    def block_of(ref, layer):
        return [[ref[i, j, layer] for j in range(3)] for i in range(3)]

    for copy in loads:
        copy.wait()
    for x in range(rows):
        maskf[x] = mask_ref[pl.ds(x, SUB, stride=rows), :].astype(jnp.float32)

    def load_layer(l, carry):
        for c in range(3):
            for x in range(rows):
                value = magnet_ref[c, l, pl.ds(x, SUB, stride=rows), :]
                base[x, l, c] = value
                field[x, l, c] = value
                masked[0, x, 1 + l, c] = value * maskf[x]
        return carry

    lax.fori_loop(0, layers, load_layer, 0)

    def unit(offset, c):
        return (lane == offset + c).astype(jnp.float32)

    zeros = jnp.zeros((SUB, LANES), jnp.float32)

    def unit_sweep(start, count, inject, finish):
        def down(i, y):
            y = [
                jnp.where(lane // 16 == 1, jnp.where(i == inject, unit(16, c), y[c]), y[c])
                for c in range(3)
            ]
            y = apply(block_of(piv_ref, start + i), apply(block_of(low_ref, start + i), y))
            y = [-y[c] for c in range(3)]
            for c in range(3):
                unit_y[i, c] = y[c]
            return tuple(y)

        last = lax.fori_loop(0, count, down, tuple(unit(0, c) for c in range(3)))

        def up(k, s):
            i = count - 1 - k
            s = apply(block_of(up_ref, start + i), s)
            return tuple(unit_y[i, c] - s[c] for c in range(3))

        mid = lax.fori_loop(0, count - finish, up, tuple(unit(32, c) for c in range(3)))
        first = lax.fori_loop(count - finish, count, up, mid)
        return last, mid, first

    def splat(slot, vec, offset):
        for r in range(3):
            for j in range(3):
                coef[slot, r * 3 + j] = jnp.broadcast_to(
                    vec[r][:, offset + j : offset + j + 1], (SUB, LANES)
                )

    def matrix(slot):
        return [[coef[slot, r * 3 + j] for j in range(3)] for r in range(3)]

    def unit_matrices():
        last, _, first = unit_sweep(first_layer, layers, 0, 0)
        splat(0, last, 0)
        splat(1, first, 0)
        splat(2, first, 32)
        _, mid, first = unit_sweep(2 * layers, 2 * layers, layers, layers)
        splat(3, first, 0)
        splat(4, mid, 16)

    def remote(slot, src, dst, device, out_slot=None):
        return pltpu.make_async_remote_copy(
            src_ref=src,
            dst_ref=dst,
            send_sem=send_sem.at[slot if out_slot is None else out_slot],
            recv_sem=recv_sem.at[slot],
            device_id=device,
            device_id_type=MESH,
        )

    def coefficient(ref, l):
        return ref[mat_ref[l]]

    nothing = tuple(jnp.zeros((rows, SUB, LANES), jnp.float32) for _ in range(3))
    for stage in range(2):
        for c in range(3):
            masked[stage, :, 0, c] = nothing[c]
            masked[stage, :, layers + 1, c] = nothing[c]

    for stage in range(2):
        slot = 8 * stage
        to_left = remote(
            slot, masked.at[stage, 0:2, 1 : layers + 1], halo_hi.at[stage], (depth_id, left)
        )
        to_right = remote(
            slot + 1,
            masked.at[stage, rows - 2 : rows, 1 : layers + 1],
            halo_lo.at[stage],
            (depth_id, right),
        )
        top = masked.at[stage, :, layers]
        edge_up = remote(slot + 2, top, edge_lo.at[stage], (above, plane_id))
        edge_down = remote(
            slot + 3, masked.at[stage, :, 1], edge_hi.at[stage], (below, plane_id)
        )
        mine_out = state_out.at[stage]
        mine_in = state_in.at[stage]
        send_first_up = remote(slot + 4, mine_out.at[0], mine_in.at[0], (above, plane_id))
        send_first_down = remote(slot + 4, mine_out.at[1], mine_in.at[0], (below, plane_id))
        across_up = remote(slot + 5, mine_out.at[2], mine_in.at[1], (above, plane_id))
        across_down = remote(slot + 5, mine_out.at[2], mine_in.at[1], (below, plane_id))
        back_down = remote(slot + 6, mine_out.at[5], mine_in.at[2], (below, plane_id))
        back_up = remote(slot + 6, mine_out.at[5], mine_in.at[2], (above, plane_id))
        hop_edge = remote(16, top, relay_in.at[0], (1, relay))
        hop_state = remote(17, mine_out.at[2], relay_in.at[1], (1, relay))
        pass_edge = remote(2, relay_in.at[0], edge_lo.at[0], (2, relay), 18)
        pass_state = remote(5, relay_in.at[1], state_in.at[0, 1], (2, relay), 19)

        def start_edges():
            @pl.when(has_below)
            def _():
                edge_down.start()

            @pl.when(jnp.logical_or(is0, is2))
            def _():
                edge_up.start()

            @pl.when(is1)
            def _():
                if stage == 0:
                    hop_edge.start()
                else:
                    edge_up.start()

        def sources(l):
            beta = coefficient(source_ref, l)
            return [beta * field[:, l, c] for c in range(3)]

        def down(l, y):
            t = sub3(sources(l), apply(block_of(low_ref, first_layer + l), y))
            y = apply(block_of(piv_ref, first_layer + l), t)
            for c in range(3):
                sweep[:, l, c] = y[c]
            return tuple(y)

        def up(k, s):
            l = layers - 1 - k
            s = apply(block_of(up_ref, first_layer + l), s)
            return tuple(sweep[:, l, c] - s[c] for c in range(3))

        def read(ref, index):
            return [ref[index, :, c] for c in range(3)]

        def write(index, value):
            for c in range(3):
                mine_out[index, :, c] = value[c]

        def start_halos():
            if stage == 1:
                to_left.start()
                to_right.start()
                return

            @pl.when(jnp.logical_not(wrap_left))
            def _():
                to_left.start()

            @pl.when(jnp.logical_not(wrap_right))
            def _():
                to_right.start()

        if stage == 1:

            @pl.when(jnp.logical_not(upper))
            def _():
                start_halos()

            start_edges()
        end = lax.fori_loop(0, layers, down, nothing)
        write(0, end)

        @pl.when(is0)
        def _():
            send_first_up.start()

        if stage == 0:
            start_halos()
            start_edges()

            @pl.when(post)
            def _():
                for group, first in ((depth_id, 2), (depth_id + 2, 4)):
                    pl.semaphore_wait(ready_sem.at[first], 1)
                    pl.semaphore_wait(ready_sem.at[first + 1], 1)
                    tell(6, (group, turn(-post_place - 1)))
                    tell(6, (group, turn(-post_place)))

        begin = lax.fori_loop(0, layers, up, nothing)
        write(1, begin)

        @pl.when(is3)
        def _():
            send_first_down.start()

        write(3, nothing)
        write(4, nothing)
        if stage == 0:
            unit_matrices()

        @pl.when(is1)
        def _():
            send_first_up.wait_recv()
            outer = read(mine_in, 0)
            write(3, outer)
            write(2, add3(read(mine_out, 0), apply(matrix(0), outer)))
            if stage == 0:
                hop_state.start()
            else:
                across_up.start()

        @pl.when(is2)
        def _():
            send_first_down.wait_recv()
            outer = read(mine_in, 0)
            inner_s = add3(outer, apply(matrix(4), read(mine_out, 0)))
            write(2, add3(read(mine_out, 1), apply(matrix(2), inner_s)))
            across_down.start()

        if stage == 0:
            flat = (sublane * LANES + lane) * K1
            offset = stream_ref[0] * K2 + count_ref[0] * K3

            def noise_layer(l, carry):
                theta = coefficient(theta_ref, l)
                for c in range(3):
                    for x in range(rows):
                        q = c * total_layers + first_layer + l
                        q = q * total_rows + plane_id * rows + x
                        h = flat + ((q * (SUB * LANES)) * K1 + offset)
                        h = h ^ shift_right(h, 16)
                        h = h * K1
                        h = h ^ shift_right(h, 15)
                        h = h * K2
                        h = h ^ shift_right(h, 16)
                        h = (h & 65535).astype(jnp.float32)
                        noise[x, l, c] = theta * (h * (1.0 / 32767.5) - 1.0)
                return carry

            lax.fori_loop(0, layers, noise_layer, 0)

            @pl.when(jnp.logical_or(wrap_left, wrap_right))
            def _():
                pl.semaphore_wait(ready_sem.at[6], 1)

                @pl.when(wrap_left)
                def _():
                    to_left.start()

                @pl.when(wrap_right)
                def _():
                    to_right.start()

            @pl.when(is1)
            def _():
                hop_edge.wait_recv()
                pl.semaphore_wait(ready_sem.at[1], 1)
                pass_edge.start()
                hop_state.wait_recv()
                pass_state.start()

        if stage == 1:

            @pl.when(upper)
            def _():
                start_halos()

        def settle():
            lax.fori_loop(0, layers, down, tuple(read(mine_out, 3)))

        def rest_layer(l, carry):
            stiff = coefficient(stiff_ref, l)
            aniso = coefficient(aniso_ref, l)
            for c in range(3):
                mine = [masked[stage, x, 1 + l, c] for x in range(rows)]
                for x in range(rows):
                    w = mine[x]
                    prev = pltpu.roll(w, 1, axis=0)
                    after = pltpu.roll(w, SUB - 1, axis=0)
                    near = pltpu.roll(jnp.where(lane == LANES - 1, prev, w), 1, axis=1)
                    near += pltpu.roll(jnp.where(lane == 0, after, w), LANES - 1, axis=1)
                    far_sum = pltpu.roll(jnp.where(lane >= LANES - 2, prev, w), 2, axis=1)
                    far_sum += pltpu.roll(jnp.where(lane < 2, after, w), LANES - 2, axis=1)
                    for other in range(rows):
                        if abs(other - x) == 1:
                            near += mine[other]
                        elif abs(other - x) == 2:
                            far_sum += mine[other]
                    planar = (4.0 / 3.0) * near - (1.0 / 12.0) * far_sum
                    vertical = masked[stage, x, 2 + l, c] + masked[stage, x, l, c]
                    h = stiff * (planar + 0.5 * vertical) + noise[x, l, c]
                    if c == 2:
                        h += aniso * field[x, l, c]
                    rest[x, l, c] = h
            return carry

        lax.fori_loop(0, layers, rest_layer, 0)

        @pl.when(is2)
        def _():
            across_up.wait_recv()
            inflow = read(mine_in, 1)
            write(3, inflow)
            end_y = add3(read(mine_out, 0), apply(matrix(0), inflow))
            write(5, end_y)
            back_up.start()
            write(4, add3(read(mine_in, 0), apply(matrix(4), end_y)))
            settle()

        @pl.when(is3)
        def _():
            back_up.wait_recv()
            write(3, read(mine_in, 2))
            settle()

        @pl.when(jnp.logical_not(upper))
        def _():
            settle()

        @pl.when(is1)
        def _():
            across_down.wait_recv()
            outer_s = add3(read(mine_in, 1), apply(matrix(3), read(mine_out, 2)))
            write(4, outer_s)
            first_s = add3(read(mine_out, 1), apply(matrix(1), read(mine_out, 3)))
            write(5, add3(first_s, apply(matrix(2), outer_s)))
            back_down.start()

        to_right.wait_recv()
        to_left.wait_recv()

        def halo_layer(l, carry):
            stiff = coefficient(stiff_ref, l)
            one = stiff * (4.0 / 3.0)
            two = stiff * (-1.0 / 12.0)
            for c in range(3):
                lows = [halo_lo[stage, i, l, c] for i in range(2)]
                highs = [halo_hi[stage, i, l, c] for i in range(2)]
                rest[0, l, c] += one * lows[1] + two * lows[0]
                rest[1, l, c] += two * lows[1]
                rest[rows - 1, l, c] += one * highs[0] + two * highs[1]
                rest[rows - 2, l, c] += two * highs[0]
            return carry

        lax.fori_loop(0, layers, halo_layer, 0)

        @pl.when(has_below)
        def _():
            edge_up.wait_recv()
            half_stiff = 0.5 * coefficient(stiff_ref, 0)
            for c in range(3):
                rest[:, 0, c] += half_stiff * edge_lo[stage, :, c]

        @pl.when(has_above)
        def _():
            edge_down.wait_recv()
            half_stiff = 0.5 * coefficient(stiff_ref, layers - 1)
            for c in range(3):
                rest[:, layers - 1, c] += half_stiff * edge_hi[stage, :, c]

        @pl.when(is0)
        def _():
            back_down.wait_recv()
            write(4, read(mine_in, 2))

        def finish_layer(k, s):
            l = layers - 1 - k
            s = apply(block_of(up_ref, first_layer + l), s)
            s = [sweep[:, l, c] - s[c] for c in range(3)]
            alpha = coefficient(damp_ref, l)
            damp = jnp.full((SUB, LANES), alpha, jnp.float32)
            scale = -1.0 / (1.0 + damp * damp)
            for x in range(rows):
                v = [field[x, l, c] for c in range(3)]
                h = [rest[x, l, c] + 0.5 * s[c][x] for c in range(3)]
                torque = cross(v, h)
                twice = cross(v, torque)
                factor = scale * maskf[x]
                change = [(torque[c] + alpha * twice[c]) * factor for c in range(3)]
                start = [base[x, l, c] for c in range(3)]
                if stage == 0:
                    moved = [start[c] + 0.03 * change[c] for c in range(3)]
                else:
                    moved = [start[c] + 0.015 * change[c] for c in range(3)]
                norm = moved[0] * moved[0] + moved[1] * moved[1] + moved[2] * moved[2]
                inverse = lax.rsqrt(norm)
                for c in range(3):
                    if stage == 0:
                        value = moved[c] * inverse
                        field[x, l, c] = value
                        masked[1, x, 1 + l, c] = value * maskf[x]
                        base[x, l, c] = start[c] + 0.015 * change[c]
                    else:
                        next_ref[c, l, pl.ds(x, SUB, stride=rows), :] = moved[c] * inverse
                        accum_ref[c, l, pl.ds(x, SUB, stride=rows), :] = s[c][x]
            return tuple(s)

        lax.fori_loop(0, layers, finish_layer, tuple(read(mine_out, 4)))
        if stage == 0:

            @pl.when(is1)
            def _():
                pl.semaphore_wait(ready_sem.at[0], 1)

        if stage == 1:
            drains.append((to_left, to_right, edge_up, edge_down))
        else:
            drains = [(to_left, to_right, edge_up, edge_down)]
        ends = [send_first_up, send_first_down, across_up, across_down, back_down, back_up]
        drains[-1] = drains[-1] + tuple(ends) + (hop_edge, hop_state, pass_edge, pass_state)

    for stage, copies in enumerate(drains):
        (to_left, to_right, edge_up, edge_down, first_up, first_down, across_up, across_down,
         back_down, back_up, hop_edge, hop_state, pass_edge, pass_state) = copies
        to_left.wait_send()
        to_right.wait_send()

        @pl.when(has_below)
        def _():
            edge_down.wait_send()

        @pl.when(jnp.logical_or(is0, is2))
        def _():
            edge_up.wait_send()

        @pl.when(is0)
        def _():
            first_up.wait_send()

        @pl.when(is3)
        def _():
            first_down.wait_send()

        @pl.when(is1)
        def _():
            back_down.wait_send()
            if stage == 0:
                for copy in (hop_edge, hop_state, pass_edge, pass_state):
                    copy.wait_send()
            else:
                edge_up.wait_send()
                across_up.wait_send()

        @pl.when(is2)
        def _():
            across_down.wait_send()
            back_up.wait_send()


def place_out(next_vmem, accum_vmem, next_hbm, accum_hbm, sem):
    copies = [
        pltpu.make_async_copy(next_vmem, next_hbm, sem.at[0]),
        pltpu.make_async_copy(accum_vmem, accum_hbm, sem.at[1]),
    ]
    for copy in copies:
        copy.start()
    for copy in copies:
        copy.wait()


def local(magnet, mask, *small):
    layers, rows, width = magnet.shape[1:]
    tiles = width // LANES

    def split(a):
        lead = a.shape[:-2]
        a = a.reshape(*lead, rows, tiles, LANES)
        return jnp.swapaxes(a, -3, -2).reshape(*lead, rows * tiles, LANES)

    def join(a):
        lead = a.shape[:-2]
        a = a.reshape(*lead, tiles, rows, LANES)
        return jnp.swapaxes(a, -3, -2).reshape(*lead, rows, width)

    small = list(small)
    for i in (6, 7, 8):
        small[i] = jnp.transpose(small[i], (1, 2, 0))
    vmem = pl.BlockSpec(memory_space=pltpu.VMEM)
    hbm = pl.BlockSpec(memory_space=pltpu.MemorySpace.HBM)
    operands = [split(magnet), split(mask), *small[:9]]
    operands = [pltpu.with_memory_space_constraint(a, pltpu.MemorySpace.HBM) for a in operands]
    held = [pltpu.VMEM(a.shape, a.dtype) for a in operands[:2]]
    held += [pltpu.SMEM(a.shape, a.dtype) for a in operands[2:]]
    shape = jax.ShapeDtypeStruct((3, layers, rows * tiles, LANES), jnp.float32)
    f32 = jnp.float32
    full = (rows, layers, 3, SUB, LANES)
    state = (rows, 3, SUB, LANES)
    outs = pl.pallas_call(
        functools.partial(kernel, layers, rows),
        out_shape=(shape, shape),
        in_specs=[hbm] * len(operands) + [pl.BlockSpec(memory_space=pltpu.SMEM)] * 2,
        out_specs=(vmem, vmem),
        scratch_shapes=held + [
            pltpu.VMEM(full, f32),
            pltpu.VMEM(full, f32),
            pltpu.VMEM((2, rows, layers + 2, 3, SUB, LANES), f32),
            pltpu.VMEM(full, f32),
            pltpu.VMEM(full, f32),
            pltpu.VMEM(full, f32),
            pltpu.VMEM((rows, SUB, LANES), f32),
            pltpu.VMEM((5, 9, SUB, LANES), f32),
            pltpu.VMEM((2 * layers, 3, SUB, LANES), f32),
            pltpu.VMEM((2, 2, layers, 3, SUB, LANES), f32),
            pltpu.VMEM((2, 2, layers, 3, SUB, LANES), f32),
            pltpu.VMEM((2, *state), f32),
            pltpu.VMEM((2, *state), f32),
            pltpu.VMEM((2, 6, *state), f32),
            pltpu.VMEM((2, 3, *state), f32),
            pltpu.VMEM((2, *state), f32),
            pltpu.SemaphoreType.DMA((len(operands),)),
            pltpu.SemaphoreType.DMA((20,)),
            pltpu.SemaphoreType.DMA((20,)),
            pltpu.SemaphoreType.REGULAR((7,)),
        ],
        compiler_params=pltpu.CompilerParams(
            collective_id=0, has_side_effects=True, vmem_limit_bytes=32 << 20
        ),
    )(*operands, *small[9:])
    outs = [pltpu.with_memory_space_constraint(a, pltpu.MemorySpace.VMEM) for a in outs]
    outs = pl.pallas_call(
        place_out,
        out_shape=(shape, shape),
        in_specs=[vmem, vmem],
        out_specs=(hbm, hbm),
        scratch_shapes=[pltpu.SemaphoreType.DMA((2,))],
        compiler_params=pltpu.CompilerParams(has_side_effects=False),
    )(*outs)
    return tuple(join(a) for a in outs)


def solution(mesh):
    placed = (P(None, "depth", "plane", None), P("plane", None), P("depth")) + (P(),) * 10
    out = P(None, "depth", "plane", None)
    return jax.shard_map(
        local, mesh=mesh, in_specs=placed, out_specs=(out, out), check_vma=False
    )
```

```python
import functools

import jax
import jax.numpy as jnp
from jax import lax
from jax.experimental import pallas as pl
from jax.experimental.pallas import tpu as pltpu
from jax.sharding import PartitionSpec as P

MESH = pl.DeviceIdType.MESH
LANES = 128
SUB = 8
K1 = 739982445
K2 = 695872825
K3 = 1597334677


def cross(a, b):
    return [a[1] * b[2] - a[2] * b[1], a[2] * b[0] - a[0] * b[2], a[0] * b[1] - a[1] * b[0]]


def apply(block, vec):
    return [block[r][0] * vec[0] + block[r][1] * vec[1] + block[r][2] * vec[2] for r in range(3)]


def sub3(a, b):
    return [a[c] - b[c] for c in range(3)]


def add3(a, b):
    return [a[c] + b[c] for c in range(3)]


def shift_right(value, amount):
    return lax.shift_right_logical(value, jnp.full(value.shape, amount, jnp.int32))


def kernel(
    layers,
    rows,
    magnet_hbm,
    mask_hbm,
    mat_hbm,
    stiff_hbm,
    aniso_hbm,
    damp_hbm,
    source_hbm,
    theta_hbm,
    piv_hbm,
    low_hbm,
    up_hbm,
    stream_ref,
    count_ref,
    next_ref,
    accum_ref,
    magnet_ref,
    mask_ref,
    mat_ref,
    stiff_ref,
    aniso_ref,
    damp_ref,
    source_ref,
    theta_ref,
    piv_ref,
    low_ref,
    up_ref,
    base,
    field,
    masked,
    noise,
    rest,
    sweep,
    maskf,
    coef,
    unit_y,
    halo_lo,
    halo_hi,
    edge_lo,
    edge_hi,
    state_out,
    state_in,
    relay_in,
    load_sem,
    send_sem,
    recv_sem,
    ready_sem,
):
    depth_id = lax.axis_index("depth")
    plane_id = lax.axis_index("plane")
    depth_count = lax.axis_size("depth")
    plane_count = lax.axis_size("plane")
    total_layers = layers * depth_count
    total_rows = rows * plane_count
    left = lax.rem(plane_id + plane_count - 1, plane_count)
    right = lax.rem(plane_id + 1, plane_count)
    above = depth_id + 1
    below = depth_id - 1
    has_below = depth_id > 0
    has_above = depth_id < depth_count - 1
    first_layer = depth_id * layers

    is0, is1, is2, is3 = (depth_id == k for k in range(4))
    mate = depth_id + 1 - 2 * lax.rem(depth_id, 2)
    half_run = 16 if plane_count % 32 == 0 else plane_count // 2
    run = 2 * half_run
    place = lax.rem(plane_id, run)
    relay = plane_id + half_run - 2 * half_run * (place // half_run)
    far = jnp.logical_or(place == 0, place == run - 1)
    upper = depth_id >= 2

    barrier = pltpu.get_barrier_semaphore()

    def greet(device):
        pl.semaphore_signal(barrier, inc=1, device_id=device, device_id_type=MESH)

    @pl.when(is1)
    def _():
        greet((2, plane_id))
        greet((2, relay))
        greet((1, relay))

    greet((mate, plane_id))
    greet((depth_id, left))
    greet((depth_id, right))
    expected = 3 + is1.astype(jnp.int32) + 2 * is2.astype(jnp.int32)

    small_hbm = (
        mat_hbm, stiff_hbm, aniso_hbm, damp_hbm, source_hbm, theta_hbm,
        piv_hbm, low_hbm, up_hbm,
    )
    small_refs = (
        mat_ref, stiff_ref, aniso_ref, damp_ref, source_ref, theta_ref,
        piv_ref, low_ref, up_ref,
    )
    loads = [
        pltpu.make_async_copy(magnet_hbm, magnet_ref, load_sem.at[0]),
        pltpu.make_async_copy(mask_hbm, mask_ref, load_sem.at[1]),
    ]
    for i, (src, dst) in enumerate(zip(small_hbm, small_refs)):
        loads.append(pltpu.make_async_copy(src, dst, load_sem.at[2 + i]))
    for copy in loads:
        copy.start()

    def meet():
        pl.semaphore_wait(barrier, expected)

        @pl.when(is2)
        def _():
            for i, other in enumerate((plane_id, relay)):
                pl.semaphore_signal(
                    ready_sem.at[i], inc=1, device_id=(1, other), device_id_type=MESH
                )

    @pl.when(jnp.logical_not(far))
    def _():
        meet()

    lane = lax.broadcasted_iota(jnp.int32, (SUB, LANES), 1)
    sublane = lax.broadcasted_iota(jnp.int32, (SUB, LANES), 0)

    def block_of(ref, layer):
        return [[ref[i, j, layer] for j in range(3)] for i in range(3)]

    for copy in loads:
        copy.wait()
    for x in range(rows):
        maskf[x] = mask_ref[pl.ds(x, SUB, stride=rows), :].astype(jnp.float32)

    def load_layer(l, carry):
        for c in range(3):
            for x in range(rows):
                value = magnet_ref[c, l, pl.ds(x, SUB, stride=rows), :]
                base[x, l, c] = value
                field[x, l, c] = value
                masked[0, x, 1 + l, c] = value * maskf[x]
        return carry

    lax.fori_loop(0, layers, load_layer, 0)

    def unit(offset, c):
        return (lane == offset + c).astype(jnp.float32)

    zeros = jnp.zeros((SUB, LANES), jnp.float32)

    def unit_sweep(start, count, inject, finish):
        def down(i, y):
            y = [
                jnp.where(lane // 16 == 1, jnp.where(i == inject, unit(16, c), y[c]), y[c])
                for c in range(3)
            ]
            y = apply(block_of(piv_ref, start + i), apply(block_of(low_ref, start + i), y))
            y = [-y[c] for c in range(3)]
            for c in range(3):
                unit_y[i, c] = y[c]
            return tuple(y)

        last = lax.fori_loop(0, count, down, tuple(unit(0, c) for c in range(3)))

        def up(k, s):
            i = count - 1 - k
            s = apply(block_of(up_ref, start + i), s)
            return tuple(unit_y[i, c] - s[c] for c in range(3))

        mid = lax.fori_loop(0, count - finish, up, tuple(unit(32, c) for c in range(3)))
        first = lax.fori_loop(count - finish, count, up, mid)
        return last, mid, first

    def splat(slot, vec, offset):
        for r in range(3):
            for j in range(3):
                coef[slot, r * 3 + j] = jnp.broadcast_to(
                    vec[r][:, offset + j : offset + j + 1], (SUB, LANES)
                )

    def matrix(slot):
        return [[coef[slot, r * 3 + j] for j in range(3)] for r in range(3)]

    def unit_matrices():
        last, _, first = unit_sweep(first_layer, layers, 0, 0)
        splat(0, last, 0)
        splat(1, first, 0)
        splat(2, first, 32)
        _, mid, first = unit_sweep(2 * layers, 2 * layers, layers, layers)
        splat(3, first, 0)
        splat(4, mid, 16)

    def remote(slot, src, dst, device, out_slot=None):
        return pltpu.make_async_remote_copy(
            src_ref=src,
            dst_ref=dst,
            send_sem=send_sem.at[slot if out_slot is None else out_slot],
            recv_sem=recv_sem.at[slot],
            device_id=device,
            device_id_type=MESH,
        )

    def coefficient(ref, l):
        return ref[mat_ref[l]]

    nothing = tuple(jnp.zeros((rows, SUB, LANES), jnp.float32) for _ in range(3))
    for stage in range(2):
        for c in range(3):
            masked[stage, :, 0, c] = nothing[c]
            masked[stage, :, layers + 1, c] = nothing[c]

    for stage in range(2):
        slot = 8 * stage
        to_left = remote(
            slot, masked.at[stage, 0:2, 1 : layers + 1], halo_hi.at[stage], (depth_id, left)
        )
        to_right = remote(
            slot + 1,
            masked.at[stage, rows - 2 : rows, 1 : layers + 1],
            halo_lo.at[stage],
            (depth_id, right),
        )
        top = masked.at[stage, :, layers]
        edge_up = remote(slot + 2, top, edge_lo.at[stage], (above, plane_id))
        edge_down = remote(
            slot + 3, masked.at[stage, :, 1], edge_hi.at[stage], (below, plane_id)
        )
        mine_out = state_out.at[stage]
        mine_in = state_in.at[stage]
        send_first_up = remote(slot + 4, mine_out.at[0], mine_in.at[0], (above, plane_id))
        send_first_down = remote(slot + 4, mine_out.at[1], mine_in.at[0], (below, plane_id))
        across_up = remote(slot + 5, mine_out.at[2], mine_in.at[1], (above, plane_id))
        across_down = remote(slot + 5, mine_out.at[2], mine_in.at[1], (below, plane_id))
        back_down = remote(slot + 6, mine_out.at[5], mine_in.at[2], (below, plane_id))
        back_up = remote(slot + 6, mine_out.at[5], mine_in.at[2], (above, plane_id))
        hop_edge = remote(16, top, relay_in.at[0], (1, relay))
        hop_state = remote(17, mine_out.at[2], relay_in.at[1], (1, relay))
        pass_edge = remote(2, relay_in.at[0], edge_lo.at[0], (2, relay), 18)
        pass_state = remote(5, relay_in.at[1], state_in.at[0, 1], (2, relay), 19)

        def start_edges():
            @pl.when(has_below)
            def _():
                edge_down.start()

            @pl.when(jnp.logical_or(is0, is2))
            def _():
                edge_up.start()

            @pl.when(is1)
            def _():
                if stage == 0:
                    hop_edge.start()
                else:
                    edge_up.start()

        def sources(l):
            beta = coefficient(source_ref, l)
            return [beta * field[:, l, c] for c in range(3)]

        def down(l, y):
            t = sub3(sources(l), apply(block_of(low_ref, first_layer + l), y))
            y = apply(block_of(piv_ref, first_layer + l), t)
            for c in range(3):
                sweep[:, l, c] = y[c]
            return tuple(y)

        def up(k, s):
            l = layers - 1 - k
            s = apply(block_of(up_ref, first_layer + l), s)
            return tuple(sweep[:, l, c] - s[c] for c in range(3))

        def read(ref, index):
            return [ref[index, :, c] for c in range(3)]

        def write(index, value):
            for c in range(3):
                mine_out[index, :, c] = value[c]

        def start_halos():
            to_left.start()
            to_right.start()

        if stage == 1:

            @pl.when(jnp.logical_not(upper))
            def _():
                start_halos()

            start_edges()
        end = lax.fori_loop(0, layers, down, nothing)
        write(0, end)
        if stage == 0:

            @pl.when(far)
            def _():
                meet()

        @pl.when(is0)
        def _():
            send_first_up.start()

        if stage == 0:
            start_halos()
            start_edges()
        begin = lax.fori_loop(0, layers, up, nothing)
        write(1, begin)

        @pl.when(is3)
        def _():
            send_first_down.start()

        write(3, nothing)
        write(4, nothing)
        if stage == 0:
            unit_matrices()

        @pl.when(is1)
        def _():
            send_first_up.wait_recv()
            outer = read(mine_in, 0)
            write(3, outer)
            write(2, add3(read(mine_out, 0), apply(matrix(0), outer)))
            if stage == 0:
                hop_state.start()
            else:
                across_up.start()

        @pl.when(is2)
        def _():
            send_first_down.wait_recv()
            outer = read(mine_in, 0)
            inner_s = add3(outer, apply(matrix(4), read(mine_out, 0)))
            write(2, add3(read(mine_out, 1), apply(matrix(2), inner_s)))
            across_down.start()

        if stage == 0:
            flat = (sublane * LANES + lane) * K1
            offset = stream_ref[0] * K2 + count_ref[0] * K3

            def noise_layer(l, carry):
                theta = coefficient(theta_ref, l)
                for c in range(3):
                    for x in range(rows):
                        q = c * total_layers + first_layer + l
                        q = q * total_rows + plane_id * rows + x
                        h = flat + ((q * (SUB * LANES)) * K1 + offset)
                        h = h ^ shift_right(h, 16)
                        h = h * K1
                        h = h ^ shift_right(h, 15)
                        h = h * K2
                        h = h ^ shift_right(h, 16)
                        h = (h & 65535).astype(jnp.float32)
                        noise[x, l, c] = theta * (h * (1.0 / 32767.5) - 1.0)
                return carry

            lax.fori_loop(0, layers, noise_layer, 0)

            @pl.when(is1)
            def _():
                hop_edge.wait_recv()
                pl.semaphore_wait(ready_sem.at[1], 1)
                pass_edge.start()
                hop_state.wait_recv()
                pass_state.start()

        if stage == 1:

            @pl.when(upper)
            def _():
                start_halos()

        def settle():
            lax.fori_loop(0, layers, down, tuple(read(mine_out, 3)))

        def rest_layer(l, carry):
            stiff = coefficient(stiff_ref, l)
            aniso = coefficient(aniso_ref, l)
            for c in range(3):
                mine = [masked[stage, x, 1 + l, c] for x in range(rows)]
                for x in range(rows):
                    w = mine[x]
                    prev = pltpu.roll(w, 1, axis=0)
                    after = pltpu.roll(w, SUB - 1, axis=0)
                    near = pltpu.roll(jnp.where(lane == LANES - 1, prev, w), 1, axis=1)
                    near += pltpu.roll(jnp.where(lane == 0, after, w), LANES - 1, axis=1)
                    far_sum = pltpu.roll(jnp.where(lane >= LANES - 2, prev, w), 2, axis=1)
                    far_sum += pltpu.roll(jnp.where(lane < 2, after, w), LANES - 2, axis=1)
                    for other in range(rows):
                        if abs(other - x) == 1:
                            near += mine[other]
                        elif abs(other - x) == 2:
                            far_sum += mine[other]
                    planar = (4.0 / 3.0) * near - (1.0 / 12.0) * far_sum
                    vertical = masked[stage, x, 2 + l, c] + masked[stage, x, l, c]
                    h = stiff * (planar + 0.5 * vertical) + noise[x, l, c]
                    if c == 2:
                        h += aniso * field[x, l, c]
                    rest[x, l, c] = h
            return carry

        lax.fori_loop(0, layers, rest_layer, 0)

        @pl.when(is2)
        def _():
            across_up.wait_recv()
            inflow = read(mine_in, 1)
            write(3, inflow)
            end_y = add3(read(mine_out, 0), apply(matrix(0), inflow))
            write(5, end_y)
            back_up.start()
            write(4, add3(read(mine_in, 0), apply(matrix(4), end_y)))
            settle()

        @pl.when(is3)
        def _():
            back_up.wait_recv()
            write(3, read(mine_in, 2))
            settle()

        @pl.when(jnp.logical_not(upper))
        def _():
            settle()

        @pl.when(is1)
        def _():
            across_down.wait_recv()
            outer_s = add3(read(mine_in, 1), apply(matrix(3), read(mine_out, 2)))
            write(4, outer_s)
            first_s = add3(read(mine_out, 1), apply(matrix(1), read(mine_out, 3)))
            write(5, add3(first_s, apply(matrix(2), outer_s)))
            back_down.start()

        to_right.wait_recv()
        to_left.wait_recv()

        def halo_layer(l, carry):
            stiff = coefficient(stiff_ref, l)
            one = stiff * (4.0 / 3.0)
            two = stiff * (-1.0 / 12.0)
            for c in range(3):
                lows = [halo_lo[stage, i, l, c] for i in range(2)]
                highs = [halo_hi[stage, i, l, c] for i in range(2)]
                rest[0, l, c] += one * lows[1] + two * lows[0]
                rest[1, l, c] += two * lows[1]
                rest[rows - 1, l, c] += one * highs[0] + two * highs[1]
                rest[rows - 2, l, c] += two * highs[0]
            return carry

        lax.fori_loop(0, layers, halo_layer, 0)

        @pl.when(has_below)
        def _():
            edge_up.wait_recv()
            half_stiff = 0.5 * coefficient(stiff_ref, 0)
            for c in range(3):
                rest[:, 0, c] += half_stiff * edge_lo[stage, :, c]

        @pl.when(has_above)
        def _():
            edge_down.wait_recv()
            half_stiff = 0.5 * coefficient(stiff_ref, layers - 1)
            for c in range(3):
                rest[:, layers - 1, c] += half_stiff * edge_hi[stage, :, c]

        @pl.when(is0)
        def _():
            back_down.wait_recv()
            write(4, read(mine_in, 2))

        def finish_layer(k, s):
            l = layers - 1 - k
            s = apply(block_of(up_ref, first_layer + l), s)
            s = [sweep[:, l, c] - s[c] for c in range(3)]
            alpha = coefficient(damp_ref, l)
            damp = jnp.full((SUB, LANES), alpha, jnp.float32)
            scale = -1.0 / (1.0 + damp * damp)
            for x in range(rows):
                v = [field[x, l, c] for c in range(3)]
                h = [rest[x, l, c] + 0.5 * s[c][x] for c in range(3)]
                torque = cross(v, h)
                twice = cross(v, torque)
                factor = scale * maskf[x]
                change = [(torque[c] + alpha * twice[c]) * factor for c in range(3)]
                start = [base[x, l, c] for c in range(3)]
                if stage == 0:
                    moved = [start[c] + 0.03 * change[c] for c in range(3)]
                else:
                    moved = [start[c] + 0.015 * change[c] for c in range(3)]
                norm = moved[0] * moved[0] + moved[1] * moved[1] + moved[2] * moved[2]
                inverse = lax.rsqrt(norm)
                for c in range(3):
                    if stage == 0:
                        value = moved[c] * inverse
                        field[x, l, c] = value
                        masked[1, x, 1 + l, c] = value * maskf[x]
                        base[x, l, c] = start[c] + 0.015 * change[c]
                    else:
                        next_ref[c, l, pl.ds(x, SUB, stride=rows), :] = moved[c] * inverse
                        accum_ref[c, l, pl.ds(x, SUB, stride=rows), :] = s[c][x]
            return tuple(s)

        lax.fori_loop(0, layers, finish_layer, tuple(read(mine_out, 4)))
        if stage == 0:

            @pl.when(is1)
            def _():
                pl.semaphore_wait(ready_sem.at[0], 1)

        if stage == 1:
            drains.append((to_left, to_right, edge_up, edge_down))
        else:
            drains = [(to_left, to_right, edge_up, edge_down)]
        ends = [send_first_up, send_first_down, across_up, across_down, back_down, back_up]
        drains[-1] = drains[-1] + tuple(ends) + (hop_edge, hop_state, pass_edge, pass_state)

    for stage, copies in enumerate(drains):
        (to_left, to_right, edge_up, edge_down, first_up, first_down, across_up, across_down,
         back_down, back_up, hop_edge, hop_state, pass_edge, pass_state) = copies
        to_left.wait_send()
        to_right.wait_send()

        @pl.when(has_below)
        def _():
            edge_down.wait_send()

        @pl.when(jnp.logical_or(is0, is2))
        def _():
            edge_up.wait_send()

        @pl.when(is0)
        def _():
            first_up.wait_send()

        @pl.when(is3)
        def _():
            first_down.wait_send()

        @pl.when(is1)
        def _():
            back_down.wait_send()
            if stage == 0:
                for copy in (hop_edge, hop_state, pass_edge, pass_state):
                    copy.wait_send()
            else:
                edge_up.wait_send()
                across_up.wait_send()

        @pl.when(is2)
        def _():
            across_down.wait_send()
            back_up.wait_send()


def place_out(next_vmem, accum_vmem, next_hbm, accum_hbm, sem):
    copies = [
        pltpu.make_async_copy(next_vmem, next_hbm, sem.at[0]),
        pltpu.make_async_copy(accum_vmem, accum_hbm, sem.at[1]),
    ]
    for copy in copies:
        copy.start()
    for copy in copies:
        copy.wait()


def local(magnet, mask, *small):
    layers, rows, width = magnet.shape[1:]
    tiles = width // LANES

    def split(a):
        lead = a.shape[:-2]
        a = a.reshape(*lead, rows, tiles, LANES)
        return jnp.swapaxes(a, -3, -2).reshape(*lead, rows * tiles, LANES)

    def join(a):
        lead = a.shape[:-2]
        a = a.reshape(*lead, tiles, rows, LANES)
        return jnp.swapaxes(a, -3, -2).reshape(*lead, rows, width)

    small = list(small)
    for i in (6, 7, 8):
        small[i] = jnp.transpose(small[i], (1, 2, 0))
    vmem = pl.BlockSpec(memory_space=pltpu.VMEM)
    hbm = pl.BlockSpec(memory_space=pltpu.MemorySpace.HBM)
    operands = [split(magnet), split(mask), *small[:9]]
    operands = [pltpu.with_memory_space_constraint(a, pltpu.MemorySpace.HBM) for a in operands]
    held = [pltpu.VMEM(a.shape, a.dtype) for a in operands[:2]]
    held += [pltpu.SMEM(a.shape, a.dtype) for a in operands[2:]]
    shape = jax.ShapeDtypeStruct((3, layers, rows * tiles, LANES), jnp.float32)
    f32 = jnp.float32
    full = (rows, layers, 3, SUB, LANES)
    state = (rows, 3, SUB, LANES)
    outs = pl.pallas_call(
        functools.partial(kernel, layers, rows),
        out_shape=(shape, shape),
        in_specs=[hbm] * len(operands) + [pl.BlockSpec(memory_space=pltpu.SMEM)] * 2,
        out_specs=(vmem, vmem),
        scratch_shapes=held + [
            pltpu.VMEM(full, f32),
            pltpu.VMEM(full, f32),
            pltpu.VMEM((2, rows, layers + 2, 3, SUB, LANES), f32),
            pltpu.VMEM(full, f32),
            pltpu.VMEM(full, f32),
            pltpu.VMEM(full, f32),
            pltpu.VMEM((rows, SUB, LANES), f32),
            pltpu.VMEM((5, 9, SUB, LANES), f32),
            pltpu.VMEM((2 * layers, 3, SUB, LANES), f32),
            pltpu.VMEM((2, 2, layers, 3, SUB, LANES), f32),
            pltpu.VMEM((2, 2, layers, 3, SUB, LANES), f32),
            pltpu.VMEM((2, *state), f32),
            pltpu.VMEM((2, *state), f32),
            pltpu.VMEM((2, 6, *state), f32),
            pltpu.VMEM((2, 3, *state), f32),
            pltpu.VMEM((2, *state), f32),
            pltpu.SemaphoreType.DMA((len(operands),)),
            pltpu.SemaphoreType.DMA((20,)),
            pltpu.SemaphoreType.DMA((20,)),
            pltpu.SemaphoreType.REGULAR((2,)),
        ],
        compiler_params=pltpu.CompilerParams(
            collective_id=0, has_side_effects=True, vmem_limit_bytes=32 << 20
        ),
    )(*operands, *small[9:])
    outs = [pltpu.with_memory_space_constraint(a, pltpu.MemorySpace.VMEM) for a in outs]
    outs = pl.pallas_call(
        place_out,
        out_shape=(shape, shape),
        in_specs=[vmem, vmem],
        out_specs=(hbm, hbm),
        scratch_shapes=[pltpu.SemaphoreType.DMA((2,))],
        compiler_params=pltpu.CompilerParams(has_side_effects=False),
    )(*outs)
    return tuple(join(a) for a in outs)


def solution(mesh):
    placed = (P(None, "depth", "plane", None), P("plane", None), P("depth")) + (P(),) * 10
    out = P(None, "depth", "plane", None)
    return jax.shard_map(
        local, mesh=mesh, in_specs=placed, out_specs=(out, out), check_vma=False
    )
```

```python
import functools

import jax
import jax.numpy as jnp
from jax import lax
from jax.experimental import pallas as pl
from jax.experimental.pallas import tpu as pltpu
from jax.sharding import PartitionSpec as P

MESH = pl.DeviceIdType.MESH
LANES = 128
SUB = 8
K1 = 739982445
K2 = 695872825
K3 = 1597334677


def cross(a, b):
    return [a[1] * b[2] - a[2] * b[1], a[2] * b[0] - a[0] * b[2], a[0] * b[1] - a[1] * b[0]]


def apply(block, vec):
    return [block[r][0] * vec[0] + block[r][1] * vec[1] + block[r][2] * vec[2] for r in range(3)]


def sub3(a, b):
    return [a[c] - b[c] for c in range(3)]


def add3(a, b):
    return [a[c] + b[c] for c in range(3)]


def shift_right(value, amount):
    return lax.shift_right_logical(value, jnp.full(value.shape, amount, jnp.int32))


def kernel(
    layers,
    rows,
    magnet_hbm,
    mask_hbm,
    mat_hbm,
    stiff_hbm,
    aniso_hbm,
    damp_hbm,
    source_hbm,
    theta_hbm,
    piv_hbm,
    low_hbm,
    up_hbm,
    stream_ref,
    count_ref,
    next_ref,
    accum_ref,
    magnet_ref,
    mask_ref,
    mat_ref,
    stiff_ref,
    aniso_ref,
    damp_ref,
    source_ref,
    theta_ref,
    piv_ref,
    low_ref,
    up_ref,
    base,
    field,
    masked,
    noise,
    rest,
    sweep,
    maskf,
    coef,
    unit_y,
    halo_lo,
    halo_hi,
    edge_lo,
    edge_hi,
    state_out,
    state_in,
    relay_in,
    load_sem,
    send_sem,
    recv_sem,
    ready_sem,
):
    depth_id = lax.axis_index("depth")
    plane_id = lax.axis_index("plane")
    depth_count = lax.axis_size("depth")
    plane_count = lax.axis_size("plane")
    total_layers = layers * depth_count
    total_rows = rows * plane_count
    left = lax.rem(plane_id + plane_count - 1, plane_count)
    right = lax.rem(plane_id + 1, plane_count)
    above = depth_id + 1
    below = depth_id - 1
    has_below = depth_id > 0
    has_above = depth_id < depth_count - 1
    first_layer = depth_id * layers

    is0, is1, is2, is3 = (depth_id == k for k in range(4))
    mate = depth_id + 1 - 2 * lax.rem(depth_id, 2)
    half_run = 16 if plane_count % 32 == 0 else plane_count // 2
    run = 2 * half_run
    place = lax.rem(plane_id, run)
    relay = plane_id + half_run - 2 * half_run * (place // half_run)
    far = jnp.logical_or(place == 0, place == run - 1)
    upper = depth_id >= 2

    barrier = pltpu.get_barrier_semaphore()

    def greet(device):
        pl.semaphore_signal(barrier, inc=1, device_id=device, device_id_type=MESH)

    @pl.when(is1)
    def _():
        greet((2, plane_id))
        greet((2, relay))
        greet((1, relay))

    greet((mate, plane_id))
    greet((depth_id, left))
    greet((depth_id, right))
    expected = 3 + is1.astype(jnp.int32) + 2 * is2.astype(jnp.int32)

    small_hbm = (
        mat_hbm, stiff_hbm, aniso_hbm, damp_hbm, source_hbm, theta_hbm,
        piv_hbm, low_hbm, up_hbm,
    )
    small_refs = (
        mat_ref, stiff_ref, aniso_ref, damp_ref, source_ref, theta_ref,
        piv_ref, low_ref, up_ref,
    )
    loads = [
        pltpu.make_async_copy(magnet_hbm, magnet_ref, load_sem.at[0]),
        pltpu.make_async_copy(mask_hbm, mask_ref, load_sem.at[1]),
    ]
    for i, (src, dst) in enumerate(zip(small_hbm, small_refs)):
        loads.append(pltpu.make_async_copy(src, dst, load_sem.at[2 + i]))
    for copy in loads:
        copy.start()

    def meet():
        pl.semaphore_wait(barrier, expected)

        @pl.when(is2)
        def _():
            for i, other in enumerate((plane_id, relay)):
                pl.semaphore_signal(
                    ready_sem.at[i], inc=1, device_id=(1, other), device_id_type=MESH
                )

    @pl.when(jnp.logical_not(far))
    def _():
        meet()

    lane = lax.broadcasted_iota(jnp.int32, (SUB, LANES), 1)
    sublane = lax.broadcasted_iota(jnp.int32, (SUB, LANES), 0)

    def block_of(ref, layer):
        return [[ref[i, j, layer] for j in range(3)] for i in range(3)]

    for copy in loads:
        copy.wait()
    for x in range(rows):
        maskf[x] = mask_ref[pl.ds(x, SUB, stride=rows), :].astype(jnp.float32)

    def load_layer(l, carry):
        for c in range(3):
            for x in range(rows):
                value = magnet_ref[c, l, pl.ds(x, SUB, stride=rows), :]
                base[x, l, c] = value
                field[x, l, c] = value
                masked[0, x, 1 + l, c] = value * maskf[x]
        return carry

    lax.fori_loop(0, layers, load_layer, 0, unroll=2)

    def unit(offset, c):
        return (lane == offset + c).astype(jnp.float32)

    zeros = jnp.zeros((SUB, LANES), jnp.float32)

    def unit_sweep(start, count, inject, finish):
        def down(i, y):
            y = [
                jnp.where(lane // 16 == 1, jnp.where(i == inject, unit(16, c), y[c]), y[c])
                for c in range(3)
            ]
            y = apply(block_of(piv_ref, start + i), apply(block_of(low_ref, start + i), y))
            y = [-y[c] for c in range(3)]
            for c in range(3):
                unit_y[i, c] = y[c]
            return tuple(y)

        last = lax.fori_loop(0, count, down, tuple(unit(0, c) for c in range(3)), unroll=4)

        def up(k, s):
            i = count - 1 - k
            s = apply(block_of(up_ref, start + i), s)
            return tuple(unit_y[i, c] - s[c] for c in range(3))

        mid = lax.fori_loop(0, count - finish, up, tuple(unit(32, c) for c in range(3)), unroll=4)
        first = lax.fori_loop(count - finish, count, up, mid)
        return last, mid, first

    def splat(slot, vec, offset):
        for r in range(3):
            for j in range(3):
                coef[slot, r * 3 + j] = jnp.broadcast_to(
                    vec[r][:, offset + j : offset + j + 1], (SUB, LANES)
                )

    def matrix(slot):
        return [[coef[slot, r * 3 + j] for j in range(3)] for r in range(3)]

    def unit_matrices():
        last, _, first = unit_sweep(first_layer, layers, 0, 0)
        splat(0, last, 0)
        splat(1, first, 0)
        splat(2, first, 32)
        _, mid, first = unit_sweep(2 * layers, 2 * layers, layers, layers)
        splat(3, first, 0)
        splat(4, mid, 16)

    def remote(slot, src, dst, device, out_slot=None):
        return pltpu.make_async_remote_copy(
            src_ref=src,
            dst_ref=dst,
            send_sem=send_sem.at[slot if out_slot is None else out_slot],
            recv_sem=recv_sem.at[slot],
            device_id=device,
            device_id_type=MESH,
        )

    def coefficient(ref, l):
        return ref[mat_ref[l]]

    nothing = tuple(jnp.zeros((rows, SUB, LANES), jnp.float32) for _ in range(3))
    for stage in range(2):
        for c in range(3):
            masked[stage, :, 0, c] = nothing[c]
            masked[stage, :, layers + 1, c] = nothing[c]

    for stage in range(2):
        slot = 8 * stage
        to_left = remote(
            slot, masked.at[stage, 0:2, 1 : layers + 1], halo_hi.at[stage], (depth_id, left)
        )
        to_right = remote(
            slot + 1,
            masked.at[stage, rows - 2 : rows, 1 : layers + 1],
            halo_lo.at[stage],
            (depth_id, right),
        )
        top = masked.at[stage, :, layers]
        edge_up = remote(slot + 2, top, edge_lo.at[stage], (above, plane_id))
        edge_down = remote(
            slot + 3, masked.at[stage, :, 1], edge_hi.at[stage], (below, plane_id)
        )
        mine_out = state_out.at[stage]
        mine_in = state_in.at[stage]
        send_first_up = remote(slot + 4, mine_out.at[0], mine_in.at[0], (above, plane_id))
        send_first_down = remote(slot + 4, mine_out.at[1], mine_in.at[0], (below, plane_id))
        across_up = remote(slot + 5, mine_out.at[2], mine_in.at[1], (above, plane_id))
        across_down = remote(slot + 5, mine_out.at[2], mine_in.at[1], (below, plane_id))
        back_down = remote(slot + 6, mine_out.at[5], mine_in.at[2], (below, plane_id))
        back_up = remote(slot + 6, mine_out.at[5], mine_in.at[2], (above, plane_id))
        hop_edge = remote(16, top, relay_in.at[0], (1, relay))
        hop_state = remote(17, mine_out.at[2], relay_in.at[1], (1, relay))
        pass_edge = remote(2, relay_in.at[0], edge_lo.at[0], (2, relay), 18)
        pass_state = remote(5, relay_in.at[1], state_in.at[0, 1], (2, relay), 19)

        def start_edges():
            @pl.when(has_below)
            def _():
                edge_down.start()

            @pl.when(jnp.logical_or(is0, is2))
            def _():
                edge_up.start()

            @pl.when(is1)
            def _():
                if stage == 0:
                    hop_edge.start()
                else:
                    edge_up.start()

        def sources(l):
            beta = coefficient(source_ref, l)
            return [beta * field[:, l, c] for c in range(3)]

        def down(l, y):
            t = sub3(sources(l), apply(block_of(low_ref, first_layer + l), y))
            y = apply(block_of(piv_ref, first_layer + l), t)
            for c in range(3):
                sweep[:, l, c] = y[c]
            return tuple(y)

        def up(k, s):
            l = layers - 1 - k
            s = apply(block_of(up_ref, first_layer + l), s)
            return tuple(sweep[:, l, c] - s[c] for c in range(3))

        def read(ref, index):
            return [ref[index, :, c] for c in range(3)]

        def write(index, value):
            for c in range(3):
                mine_out[index, :, c] = value[c]

        def start_halos():
            to_left.start()
            to_right.start()

        if stage == 1:

            @pl.when(jnp.logical_not(upper))
            def _():
                start_halos()

            start_edges()
        end = lax.fori_loop(0, layers, down, nothing, unroll=True)
        write(0, end)
        if stage == 0:

            @pl.when(far)
            def _():
                meet()

        @pl.when(is0)
        def _():
            send_first_up.start()

        if stage == 0:
            start_halos()
            start_edges()
        begin = lax.fori_loop(0, layers, up, nothing, unroll=True)
        write(1, begin)

        @pl.when(is3)
        def _():
            send_first_down.start()

        write(3, nothing)
        write(4, nothing)
        if stage == 0:
            unit_matrices()

        @pl.when(is1)
        def _():
            send_first_up.wait_recv()
            outer = read(mine_in, 0)
            write(3, outer)
            write(2, add3(read(mine_out, 0), apply(matrix(0), outer)))
            if stage == 0:
                hop_state.start()
            else:
                across_up.start()

        @pl.when(is2)
        def _():
            send_first_down.wait_recv()
            outer = read(mine_in, 0)
            inner_s = add3(outer, apply(matrix(4), read(mine_out, 0)))
            write(2, add3(read(mine_out, 1), apply(matrix(2), inner_s)))
            across_down.start()

        if stage == 0:
            flat = (sublane * LANES + lane) * K1
            offset = stream_ref[0] * K2 + count_ref[0] * K3

            def noise_layer(l, carry):
                theta = coefficient(theta_ref, l)
                for c in range(3):
                    for x in range(rows):
                        q = c * total_layers + first_layer + l
                        q = q * total_rows + plane_id * rows + x
                        h = flat + ((q * (SUB * LANES)) * K1 + offset)
                        h = h ^ shift_right(h, 16)
                        h = h * K1
                        h = h ^ shift_right(h, 15)
                        h = h * K2
                        h = h ^ shift_right(h, 16)
                        h = (h & 65535).astype(jnp.float32)
                        noise[x, l, c] = theta * (h * (1.0 / 32767.5) - 1.0)
                return carry

            lax.fori_loop(0, layers, noise_layer, 0)

            @pl.when(is1)
            def _():
                hop_edge.wait_recv()
                pl.semaphore_wait(ready_sem.at[1], 1)
                pass_edge.start()
                hop_state.wait_recv()
                pass_state.start()

        if stage == 1:

            @pl.when(upper)
            def _():
                start_halos()

        def settle():
            lax.fori_loop(0, layers, down, tuple(read(mine_out, 3)), unroll=True)

        def rest_layer(l, carry):
            stiff = coefficient(stiff_ref, l)
            aniso = coefficient(aniso_ref, l)
            for c in range(3):
                mine = [masked[stage, x, 1 + l, c] for x in range(rows)]
                for x in range(rows):
                    w = mine[x]
                    prev = pltpu.roll(w, 1, axis=0)
                    after = pltpu.roll(w, SUB - 1, axis=0)
                    near = pltpu.roll(jnp.where(lane == LANES - 1, prev, w), 1, axis=1)
                    near += pltpu.roll(jnp.where(lane == 0, after, w), LANES - 1, axis=1)
                    far_sum = pltpu.roll(jnp.where(lane >= LANES - 2, prev, w), 2, axis=1)
                    far_sum += pltpu.roll(jnp.where(lane < 2, after, w), LANES - 2, axis=1)
                    for other in range(rows):
                        if abs(other - x) == 1:
                            near += mine[other]
                        elif abs(other - x) == 2:
                            far_sum += mine[other]
                    planar = (4.0 / 3.0) * near - (1.0 / 12.0) * far_sum
                    vertical = masked[stage, x, 2 + l, c] + masked[stage, x, l, c]
                    h = stiff * (planar + 0.5 * vertical) + noise[x, l, c]
                    if c == 2:
                        h += aniso * field[x, l, c]
                    rest[x, l, c] = h
            return carry

        lax.fori_loop(0, layers, rest_layer, 0)

        @pl.when(is2)
        def _():
            across_up.wait_recv()
            inflow = read(mine_in, 1)
            write(3, inflow)
            end_y = add3(read(mine_out, 0), apply(matrix(0), inflow))
            write(5, end_y)
            back_up.start()
            write(4, add3(read(mine_in, 0), apply(matrix(4), end_y)))
            settle()

        @pl.when(is3)
        def _():
            back_up.wait_recv()
            write(3, read(mine_in, 2))
            settle()

        @pl.when(jnp.logical_not(upper))
        def _():
            settle()

        @pl.when(is1)
        def _():
            across_down.wait_recv()
            outer_s = add3(read(mine_in, 1), apply(matrix(3), read(mine_out, 2)))
            write(4, outer_s)
            first_s = add3(read(mine_out, 1), apply(matrix(1), read(mine_out, 3)))
            write(5, add3(first_s, apply(matrix(2), outer_s)))
            back_down.start()

        to_right.wait_recv()
        to_left.wait_recv()

        def halo_layer(l, carry):
            stiff = coefficient(stiff_ref, l)
            one = stiff * (4.0 / 3.0)
            two = stiff * (-1.0 / 12.0)
            for c in range(3):
                lows = [halo_lo[stage, i, l, c] for i in range(2)]
                highs = [halo_hi[stage, i, l, c] for i in range(2)]
                rest[0, l, c] += one * lows[1] + two * lows[0]
                rest[1, l, c] += two * lows[1]
                rest[rows - 1, l, c] += one * highs[0] + two * highs[1]
                rest[rows - 2, l, c] += two * highs[0]
            return carry

        lax.fori_loop(0, layers, halo_layer, 0, unroll=2)

        @pl.when(has_below)
        def _():
            edge_up.wait_recv()
            half_stiff = 0.5 * coefficient(stiff_ref, 0)
            for c in range(3):
                rest[:, 0, c] += half_stiff * edge_lo[stage, :, c]

        @pl.when(has_above)
        def _():
            edge_down.wait_recv()
            half_stiff = 0.5 * coefficient(stiff_ref, layers - 1)
            for c in range(3):
                rest[:, layers - 1, c] += half_stiff * edge_hi[stage, :, c]

        @pl.when(is0)
        def _():
            back_down.wait_recv()
            write(4, read(mine_in, 2))

        def finish_layer(k, s):
            l = layers - 1 - k
            s = apply(block_of(up_ref, first_layer + l), s)
            s = [sweep[:, l, c] - s[c] for c in range(3)]
            alpha = coefficient(damp_ref, l)
            damp = jnp.full((SUB, LANES), alpha, jnp.float32)
            scale = -1.0 / (1.0 + damp * damp)
            for x in range(rows):
                v = [field[x, l, c] for c in range(3)]
                h = [rest[x, l, c] + 0.5 * s[c][x] for c in range(3)]
                torque = cross(v, h)
                twice = cross(v, torque)
                factor = scale * maskf[x]
                change = [(torque[c] + alpha * twice[c]) * factor for c in range(3)]
                start = [base[x, l, c] for c in range(3)]
                if stage == 0:
                    moved = [start[c] + 0.03 * change[c] for c in range(3)]
                else:
                    moved = [start[c] + 0.015 * change[c] for c in range(3)]
                norm = moved[0] * moved[0] + moved[1] * moved[1] + moved[2] * moved[2]
                inverse = lax.rsqrt(norm)
                for c in range(3):
                    if stage == 0:
                        value = moved[c] * inverse
                        field[x, l, c] = value
                        masked[1, x, 1 + l, c] = value * maskf[x]
                        base[x, l, c] = start[c] + 0.015 * change[c]
                    else:
                        next_ref[c, l, pl.ds(x, SUB, stride=rows), :] = moved[c] * inverse
                        accum_ref[c, l, pl.ds(x, SUB, stride=rows), :] = s[c][x]
            return tuple(s)

        lax.fori_loop(0, layers, finish_layer, tuple(read(mine_out, 4)), unroll=4)
        if stage == 0:

            @pl.when(is1)
            def _():
                pl.semaphore_wait(ready_sem.at[0], 1)

        if stage == 1:
            drains.append((to_left, to_right, edge_up, edge_down))
        else:
            drains = [(to_left, to_right, edge_up, edge_down)]
        ends = [send_first_up, send_first_down, across_up, across_down, back_down, back_up]
        drains[-1] = drains[-1] + tuple(ends) + (hop_edge, hop_state, pass_edge, pass_state)

    for stage, copies in enumerate(drains):
        (to_left, to_right, edge_up, edge_down, first_up, first_down, across_up, across_down,
         back_down, back_up, hop_edge, hop_state, pass_edge, pass_state) = copies
        to_left.wait_send()
        to_right.wait_send()

        @pl.when(has_below)
        def _():
            edge_down.wait_send()

        @pl.when(jnp.logical_or(is0, is2))
        def _():
            edge_up.wait_send()

        @pl.when(is0)
        def _():
            first_up.wait_send()

        @pl.when(is3)
        def _():
            first_down.wait_send()

        @pl.when(is1)
        def _():
            back_down.wait_send()
            if stage == 0:
                for copy in (hop_edge, hop_state, pass_edge, pass_state):
                    copy.wait_send()
            else:
                edge_up.wait_send()
                across_up.wait_send()

        @pl.when(is2)
        def _():
            across_down.wait_send()
            back_up.wait_send()


def place_out(next_vmem, accum_vmem, next_hbm, accum_hbm, sem):
    copies = [
        pltpu.make_async_copy(next_vmem, next_hbm, sem.at[0]),
        pltpu.make_async_copy(accum_vmem, accum_hbm, sem.at[1]),
    ]
    for copy in copies:
        copy.start()
    for copy in copies:
        copy.wait()


def local(magnet, mask, *small):
    layers, rows, width = magnet.shape[1:]
    tiles = width // LANES

    def split(a):
        lead = a.shape[:-2]
        a = a.reshape(*lead, rows, tiles, LANES)
        return jnp.swapaxes(a, -3, -2).reshape(*lead, rows * tiles, LANES)

    def join(a):
        lead = a.shape[:-2]
        a = a.reshape(*lead, tiles, rows, LANES)
        return jnp.swapaxes(a, -3, -2).reshape(*lead, rows, width)

    small = list(small)
    for i in (6, 7, 8):
        small[i] = jnp.transpose(small[i], (1, 2, 0))
    vmem = pl.BlockSpec(memory_space=pltpu.VMEM)
    hbm = pl.BlockSpec(memory_space=pltpu.MemorySpace.HBM)
    operands = [split(magnet), split(mask), *small[:9]]
    operands = [pltpu.with_memory_space_constraint(a, pltpu.MemorySpace.HBM) for a in operands]
    held = [pltpu.VMEM(a.shape, a.dtype) for a in operands[:2]]
    held += [pltpu.SMEM(a.shape, a.dtype) for a in operands[2:]]
    shape = jax.ShapeDtypeStruct((3, layers, rows * tiles, LANES), jnp.float32)
    f32 = jnp.float32
    full = (rows, layers, 3, SUB, LANES)
    state = (rows, 3, SUB, LANES)
    outs = pl.pallas_call(
        functools.partial(kernel, layers, rows),
        out_shape=(shape, shape),
        in_specs=[hbm] * len(operands) + [pl.BlockSpec(memory_space=pltpu.SMEM)] * 2,
        out_specs=(vmem, vmem),
        scratch_shapes=held + [
            pltpu.VMEM(full, f32),
            pltpu.VMEM(full, f32),
            pltpu.VMEM((2, rows, layers + 2, 3, SUB, LANES), f32),
            pltpu.VMEM(full, f32),
            pltpu.VMEM(full, f32),
            pltpu.VMEM(full, f32),
            pltpu.VMEM((rows, SUB, LANES), f32),
            pltpu.VMEM((5, 9, SUB, LANES), f32),
            pltpu.VMEM((2 * layers, 3, SUB, LANES), f32),
            pltpu.VMEM((2, 2, layers, 3, SUB, LANES), f32),
            pltpu.VMEM((2, 2, layers, 3, SUB, LANES), f32),
            pltpu.VMEM((2, *state), f32),
            pltpu.VMEM((2, *state), f32),
            pltpu.VMEM((2, 6, *state), f32),
            pltpu.VMEM((2, 3, *state), f32),
            pltpu.VMEM((2, *state), f32),
            pltpu.SemaphoreType.DMA((len(operands),)),
            pltpu.SemaphoreType.DMA((20,)),
            pltpu.SemaphoreType.DMA((20,)),
            pltpu.SemaphoreType.REGULAR((2,)),
        ],
        compiler_params=pltpu.CompilerParams(
            collective_id=0, has_side_effects=True, vmem_limit_bytes=32 << 20
        ),
    )(*operands, *small[9:])
    outs = [pltpu.with_memory_space_constraint(a, pltpu.MemorySpace.VMEM) for a in outs]
    outs = pl.pallas_call(
        place_out,
        out_shape=(shape, shape),
        in_specs=[vmem, vmem],
        out_specs=(hbm, hbm),
        scratch_shapes=[pltpu.SemaphoreType.DMA((2,))],
        compiler_params=pltpu.CompilerParams(has_side_effects=False),
    )(*outs)
    return tuple(join(a) for a in outs)


def solution(mesh):
    placed = (P(None, "depth", "plane", None), P("plane", None), P("depth")) + (P(),) * 10
    out = P(None, "depth", "plane", None)
    return jax.shard_map(
        local, mesh=mesh, in_specs=placed, out_specs=(out, out), check_vma=False
    )
```
